128 devices in a mesh: row: 8 (over x, y_lo), col: 16 (over y_hi, z, core).
Axes of the slice: x: 4, y: 4 (y_hi: 2, y_lo: 2; y = y_hi * 2 + y_lo), z: 4, core: 2. Of those that a mesh axis runs over, the one named last changes fastest.
Arguments:
- tokens: bfloat16 [16384, 2048], P(('row', 'col')), may hold values from -6 to 6
- norm_gain: float32 [2048], replicated, may hold values from 0.5 to 1.5
- router_weight: bfloat16 [2048, 64], P('row'), may hold values from -0.125 to 0.125
- expert_ids: int32 [16384, 3], P(('row', 'col')), may hold values from 0 to 63, all different within a row; in each aligned block of 128 rows (0 to 127, 128 to 255, ...) at most 8 rows name the same one
- w_gate: bfloat16 [128, 2048, 704], P(('row', 'col')), may hold values from -0.125 to 0.125
- w_up: bfloat16 [128, 2048, 704], P(('row', 'col')), may hold values from -0.125 to 0.125
- w_down: bfloat16 [128, 704, 2048], P(('row', 'col')), may hold values from -0.15625 to 0.15625
- grad_mixed: bfloat16 [16384, 2048], P(('row', 'col')), may hold values from -6 to 6
Outputs:
- mixed: bfloat16 [16384, 2048], P(('row', 'col'))
- grad_tokens: bfloat16 [16384, 2048], P(('row', 'col'))
- grad_gain: float32 [2048], replicated
- grad_router: float32 [2048, 64], P('row')
- grad_gate: bfloat16 [128, 2048, 704], P(('row', 'col'))
- grad_up: bfloat16 [128, 2048, 704], P(('row', 'col'))
- grad_down: bfloat16 [128, 704, 2048], P(('row', 'col'))
The draws below stay inside these ranges and needn't reach their ends.
Inputs may be any that keep to these rules, and one draw needn't show every extreme that they name: `expert_ids`: each row names 3 different experts; in each aligned block of 128 rows (the tokens of one device) no expert is named by more than 8 rows, a bound that some block reaches.
All inputs are finite; a program needn't handle non-finite values.
Results may differ from the reference program's by a relative error of at most 0.0083.
Values may be sent and summed in bfloat16 or wider, within the bound.
No kernel may reach another device: no remote copies, remote signals or barrier semaphores. Data moves between devices by JAX's collectives and lax.ppermute only.
A program may use at most 128 MiB of HBM per device.

```python
import math
import jax
import jax.numpy as jnp
import numpy as np
from jax import lax

D = 2048
FF = 1408
TOP = 3
TOK_DEV = 128
EXPERTS = 64
HALF_FF = 704
HALVES = 128
CAP = 8
TOKENS = 16384
N_ROW = 8
N_COL = 16


def levels(own_key, dims, shards, smallest, top_value):
    def one(dim, shards_of):
        heights = jax.random.uniform(jax.random.fold_in(jax.random.fold_in(own_key, 6), dim), (shards_of,), jnp.float32, smallest / len(shards), top_value / len(shards))
        return jnp.repeat(jnp.exp(heights), dims[dim] // shards_of).reshape((-1,) + (1,) * (len(dims) - dim - 1))

    factor_of = one(*shards[0])
    for cut in shards[1:]:
        factor_of = factor_of * one(*cut)
    return factor_of


def deal_out(rng, own, number, rows, count, top, limit, slope):
    order = jax.random.permutation(rng, count)
    packed, common = portions_of(count, rows * top, limit, slope, True), portions_of(count, rows * top, limit, slope, False)
    places = jnp.arange(count)

    def named(sizes, turn):
        used = int((sizes > 0).sum())
        fixed = max(1, used // 4)
        shifted = fixed + (places - fixed + turn * (used - fixed)) % max(1, count - fixed)
        return jnp.zeros((count,), jnp.int32).at[order[jnp.where(places < fixed, places, shifted)]].set(jnp.asarray(sizes, jnp.int32))

    sizes = jnp.where(number % 4 == 0, named(packed, number // 4), named(common, number - number // 4 - 1))
    mixed = jax.random.permutation(jax.random.fold_in(own, 3), count)
    giver, receiver = mixed[0:count // 2 * 2:2], mixed[1:count // 2 * 2:2]
    room = jnp.minimum(sizes[giver] - 1, limit - sizes[receiver]) // 2
    room = jnp.where((giver == order[0]) | (receiver == order[0]) | (sizes[receiver] == 0), 0, jnp.maximum(room, 0))
    shifted = jax.random.randint(jax.random.fold_in(own, 4), (count // 2,), 0, 1 << 20) % (room + 1)
    sizes = sizes.at[giver].add(-shifted).at[receiver].add(shifted)
    labels = jnp.searchsorted(jnp.cumsum(sizes), jnp.arange(rows * top), side="right").astype(jnp.int32)
    listing = labels.reshape(top, rows).T
    listing = listing[jax.random.permutation(jax.random.fold_in(own, 1), rows)]
    turn = jax.random.randint(jax.random.fold_in(own, 2), (rows, 1), 0, top)
    return jnp.take_along_axis(listing, (jnp.arange(top)[None, :] + turn) % top, axis=1)


def portions_of(number_of, total, bound, slope, full):
    weights = [(1 << 20) // math.isqrt(standing ** slope) + 1 for standing in range(1, number_of + 1)]
    largest = bound if full else min(bound, max(-(-total // number_of), total * weights[0] // sum(weights)))
    least = 1 if total - largest >= number_of - 1 else 0
    counts, surplus = [largest] + [least] * (number_of - 1), total - largest - least * (number_of - 1)
    while surplus > 0:
        free = [i for i in range(1, number_of) if counts[i] < largest] or [i for i in range(1, number_of) if counts[i] < bound]
        whole, remaining = sum([weights[i] for i in free]), surplus
        for i in free:
            more = min(bound - counts[i], max(1, remaining * weights[i] // whole), surplus)
            counts[i] = counts[i] + more
            surplus = surplus - more
    return np.array(counts)


def normal_values(own_key, shape, scale, bound, split=(), held_as=jnp.bfloat16):
    values = jax.random.normal(own_key, shape, jnp.float32) * scale
    if len(split) > 0:
        values = levels(own_key, shape, split, -0.22, 0.18) * values
    return jnp.clip(values, min=-bound, max=bound).astype(held_as)


def setup_inputs(seed: int = 0) -> dict:
    splits = jax.random.split(jax.random.key(seed), 9)
    tokens = normal_values(splits[0], (TOKENS, D), 1.0, 6.0, ((0, 128),))
    norm_gain = jnp.clip(jax.random.uniform(splits[1], (D,), jnp.float32, 0.5, 1.5), 0.5, 1.5)
    router_weight = normal_values(splits[2], (D, EXPERTS), D ** -0.5, 0.125, ((0, 8),))
    expert_ids_keys = jax.random.split(jax.random.fold_in(splits[3], 1), TOKENS // TOK_DEV)
    expert_ids_turns = jax.random.permutation(jax.random.fold_in(splits[3], 3), TOKENS // TOK_DEV)
    expert_ids = jax.vmap(lambda own, number: deal_out(jax.random.fold_in(splits[3], 2), own, number, TOK_DEV, EXPERTS, TOP, CAP, 1))(expert_ids_keys, expert_ids_turns).reshape((TOKENS, TOP))
    w_gate = normal_values(splits[4], (HALVES, D, HALF_FF), D ** -0.5, 0.125, ((0, 128),))
    w_up = normal_values(splits[5], (HALVES, D, HALF_FF), D ** -0.5, 0.125, ((0, 128),))
    w_down = normal_values(splits[6], (HALVES, HALF_FF, D), FF ** -0.5, 0.15625, ((0, 128),))
    grad_mixed = normal_values(splits[7], (TOKENS, D), 1.0, 6.0, ((0, 128),))
    return {"tokens": tokens, "norm_gain": norm_gain, "router_weight": router_weight, "expert_ids": expert_ids, "w_gate": w_gate, "w_up": w_up, "w_down": w_down, "grad_mixed": grad_mixed}


epsilon = 1e-06

def half_pass(slot_rows, grad_out, w_gate, w_up, w_down):
    gate_pre = jnp.dot(slot_rows, w_gate, preferred_element_type=jnp.float32)
    up_pre = jnp.dot(slot_rows, w_up, preferred_element_type=jnp.float32)
    sigmoid = jax.nn.sigmoid(gate_pre)
    swish_act = gate_pre * sigmoid
    hidden = (swish_act * up_pre).astype(jnp.bfloat16)
    partial_value = jnp.dot(hidden, w_down, preferred_element_type=jnp.float32).astype(jnp.bfloat16)
    d_hidden = lax.dot_general(grad_out, w_down, (((1,), (1,)), ((), ())), preferred_element_type=jnp.float32)
    d_gate = (d_hidden * up_pre * sigmoid * (1.0 + gate_pre * (1.0 - sigmoid))).astype(jnp.bfloat16)
    d_up = (d_hidden * swish_act).astype(jnp.bfloat16)
    backward = lax.dot_general(d_gate, w_gate, (((1,), (1,)), ((), ())), preferred_element_type=jnp.float32)
    backward = backward + lax.dot_general(d_up, w_up, (((1,), (1,)), ((), ())), preferred_element_type=jnp.float32)
    grad_rows = backward.astype(jnp.bfloat16)
    grad_wgate = lax.dot_general(slot_rows, d_gate, (((0,), (0,)), ((), ())), preferred_element_type=jnp.float32).astype(jnp.bfloat16)
    grad_wup = lax.dot_general(slot_rows, d_up, (((0,), (0,)), ((), ())), preferred_element_type=jnp.float32).astype(jnp.bfloat16)
    grad_wdown = lax.dot_general(hidden, grad_out, (((0,), (0,)), ((), ())), preferred_element_type=jnp.float32).astype(jnp.bfloat16)
    return (partial_value, grad_rows, grad_wgate, grad_wup, grad_wdown)

def slot_places(expert_ids):
    blocks = N_ROW * N_COL
    flat_ids = expert_ids.reshape(blocks, TOK_DEV * TOP)
    onehot = (flat_ids[:, :, None] == jnp.arange(EXPERTS, dtype=jnp.int32)[None, None, :]).astype(jnp.int32)
    earlier = jnp.cumsum(onehot, axis=1, dtype=jnp.int32) - onehot
    ranks = lax.optimization_barrier(jnp.sum(earlier * onehot, axis=2, dtype=jnp.int32))
    block_ids = jnp.arange(blocks, dtype=jnp.int32)[:, None]
    return (flat_ids * (blocks * CAP) + block_ids * CAP + ranks).reshape(-1).astype(jnp.int32)

def reference(tokens, norm_gain, router_weight, expert_ids, w_gate, w_up, w_down, grad_mixed):
    blocks = N_ROW * N_COL
    tokens_f = tokens.astype(jnp.float32)
    inverse = lax.rsqrt(lax.optimization_barrier(jnp.mean(tokens_f * tokens_f, axis=1, keepdims=True)) + epsilon)
    normed = tokens_f * inverse
    scaled = (normed * norm_gain).astype(jnp.bfloat16)
    logits = jnp.dot(scaled, router_weight, preferred_element_type=jnp.float32)
    scores = jax.nn.sigmoid(logits)
    chosen = (expert_ids[:, :, None] == jnp.arange(EXPERTS, dtype=jnp.int32)[None, None, :]).astype(jnp.float32)
    gate_vals = lax.optimization_barrier(jnp.sum(chosen * scores[:, None, :], axis=2))
    upstream = grad_mixed.astype(jnp.float32)
    slot_grads = (gate_vals[:, :, None] * upstream[:, None, :]).astype(jnp.bfloat16).reshape(-1, D)
    places = slot_places(expert_ids)
    slot_inputs = jnp.repeat(scaled, TOP, axis=0)
    total_rows = EXPERTS * blocks * CAP
    buffer_in = jnp.zeros((total_rows, D), jnp.bfloat16).at[places].set(slot_inputs).reshape(EXPERTS, blocks * CAP, D)
    buffer_grad = jnp.zeros((total_rows, D), jnp.bfloat16).at[places].set(slot_grads).reshape(EXPERTS, blocks * CAP, D)
    gate_halves = w_gate.reshape(EXPERTS, 2, D, HALF_FF)
    up_halves = w_up.reshape(EXPERTS, 2, D, HALF_FF)
    down_halves = w_down.reshape(EXPERTS, 2, HALF_FF, D)

    def per_expert(items):
        slot_rows, grad_out, gate_pair, up_pair, down_pair = items
        first = half_pass(slot_rows, grad_out, gate_pair[0], up_pair[0], down_pair[0])
        second = half_pass(slot_rows, grad_out, gate_pair[1], up_pair[1], down_pair[1])
        outputs = (first[0].astype(jnp.float32) + second[0].astype(jnp.float32)).astype(jnp.bfloat16)
        grad_rows = (first[1].astype(jnp.float32) + second[1].astype(jnp.float32)).astype(jnp.bfloat16)
        return (outputs, grad_rows, jnp.stack([first[2], second[2]]), jnp.stack([first[3], second[3]]), jnp.stack([first[4], second[4]]))
    expert_out, expert_grad, grad_gate, grad_up, grad_down = lax.map(per_expert, (buffer_in, buffer_grad, gate_halves, up_halves, down_halves))
    slot_out = expert_out.reshape(total_rows, D)[places].reshape(-1, TOP, D).astype(jnp.float32)
    slot_back = expert_grad.reshape(total_rows, D)[places].reshape(-1, TOP, D).astype(jnp.float32)
    mixed = (tokens_f + lax.optimization_barrier(jnp.sum(gate_vals[:, :, None] * slot_out, axis=1))).astype(jnp.bfloat16)
    grad_gates = lax.optimization_barrier(jnp.sum(slot_out * upstream[:, None, :], axis=2))
    grad_logits = (lax.optimization_barrier(jnp.sum(chosen * grad_gates[:, :, None], axis=1)) * scores * (1.0 - scores)).astype(jnp.bfloat16)
    grad_scaled = lax.optimization_barrier(jnp.sum(slot_back, axis=1)) + lax.dot_general(grad_logits, router_weight, (((1,), (1,)), ((), ())), preferred_element_type=jnp.float32)
    grad_router = lax.dot_general(scaled, grad_logits, (((0,), (0,)), ((), ())), preferred_element_type=jnp.float32)
    grad_gain = lax.optimization_barrier(jnp.sum(grad_scaled * normed, axis=0))
    grad_normed = grad_scaled * norm_gain
    grad_tokens = (upstream + inverse * (grad_normed - normed * lax.optimization_barrier(jnp.mean(grad_normed * normed, axis=1, keepdims=True)))).astype(jnp.bfloat16)
    return (mixed, grad_tokens, grad_gain, grad_router, grad_gate.reshape(2 * EXPERTS, D, HALF_FF), grad_up.reshape(2 * EXPERTS, D, HALF_FF), grad_down.reshape(2 * EXPERTS, HALF_FF, D))
```

```python
import jax
import jax.numpy as jnp
from jax import lax
from jax.experimental import pallas as pl
from jax.experimental.pallas import tpu as pltpu
from jax.sharding import Mesh
from jax.sharding import PartitionSpec as P


ROW_COL = ("row_0", "row_1", "col_0", "col_1", "col_2")
CHIPS = ("row_0", "row_1", "col_0", "col_1")
ROW = ("row_0", "row_1")
CORE = "col_2"
CAP = 8
LANES = 128
F32 = jnp.float32
BF16 = jnp.bfloat16
EPSILON = 1e-06


def dot_nn(a, b):
    return lax.dot_general(a, b, (((1,), (0,)), ((), ())), preferred_element_type=F32)


def dot_nt(a, b):
    return lax.dot_general(a, b, (((1,), (1,)), ((), ())), preferred_element_type=F32)


def dot_tn(a, b):
    return lax.dot_general(a, b, (((0,), (0,)), ((), ())), preferred_element_type=F32)


def cost(flops, bytes_accessed):
    return pl.CostEstimate(flops=int(flops), bytes_accessed=int(bytes_accessed), transcendentals=0)


def whole(shape):
    return pl.BlockSpec(shape, lambda i: (0,) * len(shape))


def one_hot_rows(rows, cols, column_of):
    row = lax.broadcasted_iota(jnp.int32, (rows, cols), 0)
    col = lax.broadcasted_iota(jnp.int32, (rows, cols), 1)
    return jnp.where(column_of(row) == col, 1.0, 0.0).astype(BF16)


def dispatch_kernel(tok_ref, gain_ref, ids_ref, router_ref, send_ref, place_ref, scaled_scr):
    step = pl.program_id(0)
    chunks, tok_count, width = scaled_scr.shape
    slots = place_ref.shape[0]
    experts = slots // CAP

    @pl.when(step == 0)
    def _():
        x = tok_ref[...].astype(F32)
        inverse = lax.rsqrt(jnp.mean(x * x, axis=1, keepdims=True) + EPSILON)
        scaled = (x * inverse * gain_ref[...]).astype(BF16)
        for c in range(chunks):
            scaled_scr[c] = scaled[:, c * width : (c + 1) * width]
        ids = ids_ref[...]
        expert = lax.broadcasted_iota(jnp.int32, (experts, tok_count), 0)
        named = jnp.zeros((experts, tok_count), F32)
        for k in range(ids.shape[0]):
            named = named + jnp.where(ids[k : k + 1, :] == expert, 1.0, 0.0)
        before = lax.broadcasted_iota(jnp.int32, (tok_count, tok_count), 0)
        after = lax.broadcasted_iota(jnp.int32, (tok_count, tok_count), 1)
        earlier = jnp.where(before < after, 1.0, 0.0).astype(BF16)
        rank = dot_nn(named.astype(BF16), earlier)
        order = (named * (rank + 1.0)).astype(BF16)
        order_of = dot_nn(one_hot_rows(slots, experts, lambda row: row // CAP), order)
        want = (lax.broadcasted_iota(jnp.int32, (slots, tok_count), 0) % CAP + 1).astype(F32)
        place_ref[...] = jnp.where(order_of == want, 1.0, 0.0).astype(BF16)

    @pl.when(step < chunks)
    def _():
        send_ref[...] = dot_nn(place_ref[...], scaled_scr[jnp.minimum(step, chunks - 1)]).astype(BF16)

    @pl.when(step == chunks)
    def _():
        extra = jnp.zeros((slots, LANES), F32)
        for j in range(router_ref.shape[1] // LANES):
            pick = one_hot_rows(slots, experts, lambda row: jnp.where(row % CAP == j, row // CAP, -1))
            extra = extra + dot_nn(pick, router_ref[:, j * LANES : (j + 1) * LANES])
        send_ref[:, :LANES] = extra.astype(BF16)


def dispatch(tokens, gain, ids, router, slots):
    tok_count, width = tokens.shape
    chunks = 4
    part = width // chunks
    return pl.pallas_call(
        dispatch_kernel,
        grid=(chunks + 1,),
        out_shape=(
            jax.ShapeDtypeStruct((slots, width + LANES), BF16),
            jax.ShapeDtypeStruct((slots, tok_count), BF16),
        ),
        in_specs=[whole((tok_count, width)), whole((1, width)), whole(ids.shape), whole(router.shape)],
        out_specs=(
            pl.BlockSpec((slots, part), lambda i: (0, i)),
            whole((slots, tok_count)),
        ),
        scratch_shapes=[pltpu.VMEM((chunks, tok_count, part), BF16)],
        compiler_params=pltpu.CompilerParams(dimension_semantics=("arbitrary",)),
        cost_estimate=cost(2 * slots * tok_count * width, 2 * slots * width * 2),
        name="dispatch_tokens",
    )(tokens, gain, ids, router)


def column_kernel(extra_ref, rc_ref):
    extra = extra_ref[...].astype(F32)
    rows_n, per_row = 8, 2
    stride = extra.shape[0] // rows_n
    parts = [extra[r * stride + j : r * stride + j + 1, :] for r in range(rows_n) for j in range(per_row)]
    rc_ref[...] = jnp.broadcast_to(jnp.concatenate(parts, axis=1), rc_ref.shape).astype(BF16)


def own_column(rows_in, width):
    rows, _ = rows_in.shape
    return pl.pallas_call(
        column_kernel,
        grid=(1,),
        out_shape=jax.ShapeDtypeStruct((LANES, width), BF16),
        in_specs=[pl.BlockSpec((rows, LANES), lambda i: (0, width // LANES))],
        out_specs=whole((LANES, width)),
        cost_estimate=cost(rows * LANES, 2 * LANES * (rows + width)),
        name="own_column",
    )(rows_in)


def place_kernel(place_ref, x_ref, send_ref):
    send_ref[...] = dot_nn(place_ref[...], x_ref[...]).astype(BF16)


def place_rows(place, x):
    slots, tok_count = place.shape
    width = x.shape[1]
    chunks = 4
    part = width // chunks
    return pl.pallas_call(
        place_kernel,
        grid=(chunks,),
        out_shape=jax.ShapeDtypeStruct((slots, width), BF16),
        in_specs=[whole((slots, tok_count)), pl.BlockSpec((tok_count, part), lambda i: (0, i))],
        out_specs=pl.BlockSpec((slots, part), lambda i: (0, i)),
        compiler_params=pltpu.CompilerParams(dimension_semantics=("arbitrary",)),
        cost_estimate=cost(2 * slots * tok_count * width, 2 * slots * width * 2),
        name="dispatch_grads",
    )(place, x)


def forward_kernel(x_ref, wg_ref, wu_ref, wd_ref, rc_ref, out_ref, hg_ref, g_ref, u_ref, gate_ref):
    x = x_ref[...]
    gate = jax.nn.sigmoid(dot_nt(x, rc_ref[...]))
    g = dot_nt(x, wg_ref[...])
    u = dot_nt(x, wu_ref[...])
    hidden = g * jax.nn.sigmoid(g) * u
    gated = (hidden * gate[:, :1]).astype(BF16)
    out_ref[...] = dot_nn(gated, wd_ref[...]).astype(BF16)
    hg_ref[...] = gated
    g_ref[...] = g
    u_ref[...] = u
    gate_ref[...] = gate


def forward(x, wg, wu, wd, rc):
    rows = x.shape[0]
    ff, width = wg.shape
    blk = 256
    row_blk = lambda n: pl.BlockSpec((blk, n), lambda i: (i, 0))
    return pl.pallas_call(
        forward_kernel,
        grid=(rows // blk,),
        out_shape=(
            jax.ShapeDtypeStruct((rows, width), BF16),
            jax.ShapeDtypeStruct((rows, ff), BF16),
            jax.ShapeDtypeStruct((rows, ff), F32),
            jax.ShapeDtypeStruct((rows, ff), F32),
            jax.ShapeDtypeStruct((rows, LANES), F32),
        ),
        in_specs=[row_blk(width), whole((ff, width)), whole((ff, width)), whole((ff, width)), whole((LANES, width))],
        out_specs=(row_blk(width), row_blk(ff), row_blk(ff), row_blk(ff), row_blk(LANES)),
        compiler_params=pltpu.CompilerParams(dimension_semantics=("arbitrary",)),
        cost_estimate=cost(6 * rows * ff * width, 6 * ff * width + 8 * rows * width),
        name="expert_forward",
    )(x, wg, wu, wd, rc)


def backward_kernel(gr_ref, g_ref, u_ref, gate_ref, wg_ref, wu_ref, wd_ref, back_ref, dg_ref, du_ref, gg_ref):
    g = g_ref[...]
    u = u_ref[...]
    s = jax.nn.sigmoid(g)
    act = g * s
    dh = dot_nt(gr_ref[...], wd_ref[...])
    inner = jnp.sum(dh * (act * u), axis=1, keepdims=True)
    gg_ref[...] = jnp.broadcast_to(inner, gg_ref.shape)
    dh = dh * gate_ref[:, :1]
    dg = (dh * u * s * (1.0 + g * (1.0 - s))).astype(BF16)
    du = (dh * act).astype(BF16)
    dg_ref[...] = dg
    du_ref[...] = du
    back_ref[...] = (dot_nn(dg, wg_ref[...]) + dot_nn(du, wu_ref[...])).astype(BF16)


def backward(gr, g, u, gate, wg, wu, wd):
    rows, width = gr.shape
    ff = wg.shape[0]
    blk = 256
    row_blk = lambda n: pl.BlockSpec((blk, n), lambda i: (i, 0))
    return pl.pallas_call(
        backward_kernel,
        grid=(rows // blk,),
        out_shape=(
            jax.ShapeDtypeStruct((rows, width), BF16),
            jax.ShapeDtypeStruct((rows, ff), BF16),
            jax.ShapeDtypeStruct((rows, ff), BF16),
            jax.ShapeDtypeStruct((rows, LANES), F32),
        ),
        in_specs=[row_blk(width), row_blk(ff), row_blk(ff), row_blk(LANES)] + [whole((ff, width))] * 3,
        out_specs=(row_blk(width), row_blk(ff), row_blk(ff), row_blk(LANES)),
        compiler_params=pltpu.CompilerParams(dimension_semantics=("arbitrary",)),
        cost_estimate=cost(6 * rows * ff * width, 6 * ff * width + 8 * rows * width),
        name="expert_backward",
    )(gr, g, u, gate, wg, wu, wd)


def join_out_kernel(mine_ref, sib_ref, out_ref):
    out_ref[...] = (mine_ref[...].astype(F32) + sib_ref[...].astype(F32)).astype(BF16)


def join_halves(mine, sib):
    rows, width = mine.shape
    blk = pl.BlockSpec((128, width), lambda i: (i, 0))
    return pl.pallas_call(
        join_out_kernel,
        grid=(rows // 128,),
        out_shape=jax.ShapeDtypeStruct((rows, width), BF16),
        in_specs=[blk, blk],
        out_specs=blk,
        compiler_params=pltpu.CompilerParams(dimension_semantics=("arbitrary",)),
        cost_estimate=cost(3 * rows * width, 6 * rows * width),
        name="join_halves",
    )(mine, sib)


def weight_grad_kernel(d0_ref, d1_ref, x0_ref, x1_ref, out_ref):
    out_ref[...] = (dot_tn(d0_ref[...], x0_ref[...]) + dot_tn(d1_ref[...], x1_ref[...])).astype(BF16)


def weight_grad(d0, d1, x0, x1, width):
    rows, ff = d0.shape
    part = 512
    col = pl.BlockSpec((rows, part), lambda i: (0, i))
    return pl.pallas_call(
        weight_grad_kernel,
        grid=(width // part,),
        out_shape=jax.ShapeDtypeStruct((ff, width), BF16),
        in_specs=[whole((rows, ff)), whole((rows, ff)), col, col],
        out_specs=pl.BlockSpec((ff, part), lambda i: (0, i)),
        compiler_params=pltpu.CompilerParams(dimension_semantics=("arbitrary",)),
        cost_estimate=cost(4 * rows * ff * width, 4 * rows * width + 2 * ff * width),
    )(d0, d1, x0, x1)


def join_kernel(mine_ref, sib_ref, gg_ref, gg_sib_ref, gate_ref, rc_ref, x_ref, back_ref, gain_scr, router_scr):
    step = pl.program_id(0)
    chunks, _, part = gain_scr.shape
    rows = back_ref.shape[0]

    @pl.when(step < chunks)
    def _():
        c = jnp.minimum(step, chunks - 1)
        gate = gate_ref[...]
        gl = ((gg_ref[...] + gg_sib_ref[...]) * gate * (1.0 - gate)).astype(BF16).astype(F32)[:, :1]
        x = x_ref[...].astype(F32)
        back = mine_ref[...].astype(F32) + sib_ref[...].astype(F32) + gl * rc_ref[:1, :].astype(F32)
        back_ref[...] = back.astype(BF16)
        gain_scr[c] = jnp.sum(x * back, axis=0, keepdims=True)
        router_scr[c] = jnp.sum(x * gl, axis=0, keepdims=True)

    @pl.when(step == chunks)
    def _():
        lanes = chunks * part // CAP
        gain = jnp.concatenate([gain_scr[c] for c in range(chunks)], axis=1)
        gain = jnp.concatenate([gain[:, j * lanes : (j + 1) * lanes] for j in range(CAP)], axis=0)
        gain = jnp.broadcast_to(gain[None], (rows // CAP, CAP, lanes)).reshape(rows, lanes)
        back_ref[:, :lanes] = gain.astype(BF16)
        router = jnp.concatenate([router_scr[c] for c in range(chunks)], axis=1)
        parts = chunks * part // LANES
        router = jnp.concatenate([router[:, j * LANES : (j + 1) * LANES] for j in range(parts)], axis=0)
        per_row = parts // 8
        pick = one_hot_rows(
            rows,
            parts,
            lambda row: jnp.where(row % CAP < per_row, row // (rows // 8) * per_row + row % CAP, -1),
        )
        back_ref[:, lanes : lanes + LANES] = dot_nn(pick, router.astype(BF16)).astype(BF16)


def join_back(mine, sib, gg, gg_sib, gate, rc, x):
    rows, width = mine.shape
    part = 512
    chunks = width // part
    at = lambda i: (0, jnp.minimum(i, chunks - 1))
    col = pl.BlockSpec((rows, part), at)
    return pl.pallas_call(
        join_kernel,
        grid=(chunks + 1,),
        out_shape=jax.ShapeDtypeStruct((rows, width + width // CAP + LANES), BF16),
        in_specs=[col, col] + [whole((rows, LANES))] * 3 + [pl.BlockSpec((LANES, part), at), col],
        out_specs=pl.BlockSpec((rows, part), lambda i: (0, i)),
        scratch_shapes=[pltpu.VMEM((chunks, 1, part), F32), pltpu.VMEM((chunks, 1, part), F32)],
        compiler_params=pltpu.CompilerParams(dimension_semantics=("arbitrary",)),
        cost_estimate=cost(10 * rows * width, 8 * rows * width),
        name="join_back",
    )(mine, sib, gg, gg_sib, gate, rc, x)


def collect_kernel(a_ref, b_ref, c_ref, out_ref):
    rows = a_ref.shape[0]
    chips = rows // CAP
    for half, ref in enumerate((a_ref, b_ref)):
        total = jnp.sum(ref[...].astype(F32).reshape(chips, CAP, LANES), axis=0)
        out_ref[:CAP, half * LANES : (half + 1) * LANES] = total
    for j in range(2):
        pick = one_hot_rows(chips, rows, lambda row: row * CAP + j)
        out_ref[CAP:, j * LANES : (j + 1) * LANES] = dot_nn(pick, c_ref[...])


def collect(rows_in, width):
    rows = rows_in.shape[0]
    first = width // LANES
    lane = lambda k: pl.BlockSpec((rows, LANES), lambda i: (0, first + k))
    return pl.pallas_call(
        collect_kernel,
        grid=(1,),
        out_shape=jax.ShapeDtypeStruct((CAP + rows // CAP, 2 * LANES), F32),
        in_specs=[lane(0), lane(1), lane(2)],
        out_specs=whole((CAP + rows // CAP, 2 * LANES)),
        cost_estimate=cost(rows * rows * LANES, 6 * rows * LANES),
        name="collect_sums",
    )(rows_in, rows_in, rows_in)


def mix_kernel(place_ref, rows_ref, tok_ref, mixed_ref, acc_ref):
    step = pl.program_id(0)
    part = dot_tn(place_ref[...], rows_ref[...])

    @pl.when(step == 0)
    def _():
        acc_ref[...] = part

    @pl.when(step > 0)
    def _():
        acc_ref[...] += part

    @pl.when(step == pl.num_programs(0) - 1)
    def _():
        mixed_ref[...] = (tok_ref[...].astype(F32) + acc_ref[...]).astype(BF16)


def mix(place, rows, tokens):
    slots, tok_count = place.shape
    width = tokens.shape[1]
    part = 128
    return pl.pallas_call(
        mix_kernel,
        grid=(slots // part,),
        out_shape=jax.ShapeDtypeStruct((tok_count, width), BF16),
        in_specs=[
            pl.BlockSpec((part, tok_count), lambda i: (i, 0)),
            pl.BlockSpec((part, width), lambda i: (i, 0)),
            whole((tok_count, width)),
        ],
        out_specs=whole((tok_count, width)),
        scratch_shapes=[pltpu.VMEM((tok_count, width), F32)],
        compiler_params=pltpu.CompilerParams(dimension_semantics=("arbitrary",)),
        cost_estimate=cost(2 * slots * tok_count * width, 2 * slots * width),
        name="mix_outputs",
    )(place, rows, tokens)


def finish_kernel(place_ref, rows_ref, tok_ref, gain_ref, up_ref, out_ref, acc_ref):
    step = pl.program_id(0)
    part = dot_tn(place_ref[...], rows_ref[...])

    @pl.when(step == 0)
    def _():
        acc_ref[...] = part

    @pl.when(step > 0)
    def _():
        acc_ref[...] += part

    @pl.when(step == pl.num_programs(0) - 1)
    def _():
        x = tok_ref[...].astype(F32)
        inverse = lax.rsqrt(jnp.mean(x * x, axis=1, keepdims=True) + EPSILON)
        normed = x * inverse
        gn = acc_ref[...] * gain_ref[...]
        out = up_ref[...].astype(F32) + inverse * (gn - normed * jnp.mean(gn * normed, axis=1, keepdims=True))
        out_ref[...] = out.astype(BF16)


def finish(place, rows, tokens, gain, upstream):
    slots, tok_count = place.shape
    width = tokens.shape[1]
    part = 128
    return pl.pallas_call(
        finish_kernel,
        grid=(slots // part,),
        out_shape=jax.ShapeDtypeStruct((tok_count, width), BF16),
        in_specs=[
            pl.BlockSpec((part, tok_count), lambda i: (i, 0)),
            pl.BlockSpec((part, width), lambda i: (i, 0)),
            whole((tok_count, width)),
            whole((1, width)),
            whole((tok_count, width)),
        ],
        out_specs=whole((tok_count, width)),
        scratch_shapes=[pltpu.VMEM((tok_count, width), F32)],
        compiler_params=pltpu.CompilerParams(dimension_semantics=("arbitrary",)),
        cost_estimate=cost(2 * slots * tok_count * width, 2 * slots * width),
        name="finish_tokens",
    )(place, rows, tokens, gain, upstream)


def across(block, axis, bit):
    count = lax.axis_size(axis)
    return lax.ppermute(block, axis, [(i, i ^ bit) for i in range(count)])


def exchange(x, experts):
    rows, width = x.shape
    return lax.all_to_all(x.reshape(experts, -1, width), CHIPS, 0, 0, tiled=True).reshape(rows, width)


def local(tokens, norm_gain, router_weight, expert_ids, w_gate, w_up, w_down, grad_mixed):
    _, width = tokens.shape
    experts = router_weight.shape[1]
    slots = experts * CAP
    gain = norm_gain.reshape(1, width)
    wg, wu, wd = w_gate[0].T, w_up[0].T, w_down[0]

    send_in, place = dispatch(tokens, gain, expert_ids.T, router_weight.T, slots)
    in_0 = exchange(send_in, experts)
    rc = own_column(in_0, width)
    send_grad = place_rows(place, grad_mixed)
    gr_0 = exchange(send_grad, experts)
    in_1 = across(in_0, CORE, 1)
    gr_1 = across(gr_0, CORE, 1)

    out_0, hg_0, g_0, u_0, gate_0 = forward(in_0, wg, wu, wd, rc)
    out_1, hg_1, g_1, u_1, gate_1 = forward(in_1, wg, wu, wd, rc)
    out_s = across(out_1, CORE, 1)
    out = join_halves(out_0, out_s)
    got_out = exchange(out, experts)
    mixed = mix(place, got_out, tokens)

    back_0, dg_0, du_0, gg_0 = backward(gr_0, g_0, u_0, gate_0, wg, wu, wd)
    back_1, dg_1, du_1, gg_1 = backward(gr_1, g_1, u_1, gate_1, wg, wu, wd)
    back_s = across(back_1, CORE, 1)
    gg_s = across(gg_1, CORE, 1)
    back = join_back(back_0, back_s, gg_0, gg_s, gate_0, rc, in_0)
    got_back = exchange(back, experts)
    grad_tokens = finish(place, got_back, tokens, gain, grad_mixed)

    grad_down = weight_grad(hg_0, hg_1, gr_0, gr_1, width)
    grad_gate = weight_grad(dg_0, dg_1, in_0, in_1, width)
    grad_up = weight_grad(du_0, du_1, in_0, in_1, width)

    sums = collect(got_back, width)
    sums = sums + across(sums, CORE, 1)
    grad_gain = sums[:CAP].reshape(width) / norm_gain
    grad_router = sums[CAP:].T
    return (
        mixed,
        grad_tokens,
        grad_gain,
        grad_router,
        grad_gate.T[None],
        grad_up.T[None],
        grad_down[None],
    )


def solution(mesh):
    finer = Mesh(mesh.devices.reshape(4, 2, 2, 4, 2), ROW_COL)
    placed = (
        P(ROW_COL, None),
        P(),
        P(ROW, None),
        P(ROW_COL, None),
        P(ROW_COL, None, None),
        P(ROW_COL, None, None),
        P(ROW_COL, None, None),
        P(ROW_COL, None),
    )
    return jax.shard_map(
        local,
        mesh=finer,
        in_specs=placed,
        out_specs=(
            P(ROW_COL, None),
            P(ROW_COL, None),
            P(),
            P(ROW, None),
            P(ROW_COL, None, None),
            P(ROW_COL, None, None),
            P(ROW_COL, None, None),
        ),
        check_vma=False,
    )
```

```python
import jax
import jax.numpy as jnp
from jax import lax
from jax.experimental import pallas as pl
from jax.experimental.pallas import tpu as pltpu
from jax.sharding import Mesh
from jax.sharding import PartitionSpec as P


ROW_COL = ("row_0", "row_1", "col_0", "col_1", "col_2")
CHIPS = ("row_0", "row_1", "col_0", "col_1")
ROW = ("row_0", "row_1")
CORE = "col_2"
CAP = 8
LANES = 128
F32 = jnp.float32
BF16 = jnp.bfloat16
EPSILON = 1e-06
KEEPING = 50 << 20


def dot_nn(a, b):
    return lax.dot_general(a, b, (((1,), (0,)), ((), ())), preferred_element_type=F32)


def dot_nt(a, b):
    return lax.dot_general(a, b, (((1,), (1,)), ((), ())), preferred_element_type=F32)


def dot_tn(a, b):
    return lax.dot_general(a, b, (((0,), (0,)), ((), ())), preferred_element_type=F32)


VMEM = pl.BlockSpec(memory_space=pltpu.VMEM)
HBM = pl.BlockSpec(memory_space=pltpu.HBM)


def in_vmem(x):
    return pltpu.with_memory_space_constraint(x, pltpu.VMEM)


def in_hbm(x):
    return pltpu.with_memory_space_constraint(x, pltpu.HBM)


def cost(flops, bytes_accessed):
    return pl.CostEstimate(flops=int(flops), bytes_accessed=int(bytes_accessed), transcendentals=0)


def whole(shape):
    return pl.BlockSpec(shape, lambda i: (0,) * len(shape))


def one_hot_rows(rows, cols, column_of):
    row = lax.broadcasted_iota(jnp.int32, (rows, cols), 0)
    col = lax.broadcasted_iota(jnp.int32, (rows, cols), 1)
    return jnp.where(column_of(row) == col, 1.0, 0.0).astype(BF16)


def dispatch_kernel(tok_ref, gain_ref, ids_ref, router_ref, send_ref, place_ref, scaled_scr):
    step = pl.program_id(0)
    chunks, tok_count, width = scaled_scr.shape
    slots = place_ref.shape[0]
    experts = slots // CAP

    @pl.when(step == 0)
    def _():
        x = tok_ref[...].astype(F32)
        inverse = lax.rsqrt(jnp.mean(x * x, axis=1, keepdims=True) + EPSILON)
        scaled = (x * inverse * gain_ref[...]).astype(BF16)
        for c in range(chunks):
            scaled_scr[c] = scaled[:, c * width : (c + 1) * width]
        ids = ids_ref[...]
        expert = lax.broadcasted_iota(jnp.int32, (experts, tok_count), 0)
        named = jnp.zeros((experts, tok_count), F32)
        for k in range(ids.shape[0]):
            named = named + jnp.where(ids[k : k + 1, :] == expert, 1.0, 0.0)
        before = lax.broadcasted_iota(jnp.int32, (tok_count, tok_count), 0)
        after = lax.broadcasted_iota(jnp.int32, (tok_count, tok_count), 1)
        earlier = jnp.where(before < after, 1.0, 0.0).astype(BF16)
        rank = dot_nn(named.astype(BF16), earlier)
        order = (named * (rank + 1.0)).astype(BF16)
        order_of = dot_nn(one_hot_rows(slots, experts, lambda row: row // CAP), order)
        want = (lax.broadcasted_iota(jnp.int32, (slots, tok_count), 0) % CAP + 1).astype(F32)
        place_ref[...] = jnp.where(order_of == want, 1.0, 0.0).astype(BF16)

    @pl.when(step < chunks)
    def _():
        send_ref[...] = dot_nn(place_ref[...], scaled_scr[jnp.minimum(step, chunks - 1)]).astype(BF16)

    @pl.when(step == chunks)
    def _():
        extra = jnp.zeros((slots, LANES), F32)
        for j in range(router_ref.shape[1] // LANES):
            pick = one_hot_rows(slots, experts, lambda row: jnp.where(row % CAP == j, row // CAP, -1))
            extra = extra + dot_nn(pick, router_ref[:, j * LANES : (j + 1) * LANES])
        send_ref[:, :LANES] = extra.astype(BF16)


def dispatch(tokens, gain, ids, router, slots):
    tok_count, width = tokens.shape
    chunks = 4
    part = width // chunks
    return pl.pallas_call(
        dispatch_kernel,
        grid=(chunks + 1,),
        out_shape=(
            jax.ShapeDtypeStruct((slots, width + LANES), BF16),
            jax.ShapeDtypeStruct((slots, tok_count), BF16),
        ),
        in_specs=[whole((tok_count, width)), whole((1, width)), whole(ids.shape), whole(router.shape)],
        out_specs=(
            pl.BlockSpec((slots, part), lambda i: (0, i)),
            whole((slots, tok_count)),
        ),
        scratch_shapes=[pltpu.VMEM((chunks, tok_count, part), BF16)],
        compiler_params=pltpu.CompilerParams(dimension_semantics=("arbitrary",)),
        cost_estimate=cost(2 * slots * tok_count * width, 2 * slots * width * 2),
        name="dispatch_tokens",
    )(tokens, gain, ids, router)


def place_kernel(place_ref, x_ref, send_ref):
    send_ref[...] = dot_nn(place_ref[...], x_ref[...]).astype(BF16)


def place_rows(place, x):
    slots, tok_count = place.shape
    width = x.shape[1]
    chunks = 4
    part = width // chunks
    return pl.pallas_call(
        place_kernel,
        grid=(chunks,),
        out_shape=jax.ShapeDtypeStruct((slots, width), BF16),
        in_specs=[whole((slots, tok_count)), pl.BlockSpec((tok_count, part), lambda i: (0, i))],
        out_specs=pl.BlockSpec((slots, part), lambda i: (0, i)),
        compiler_params=pltpu.CompilerParams(dimension_semantics=("arbitrary",)),
        cost_estimate=cost(2 * slots * tok_count * width, 2 * slots * width * 2),
        name="dispatch_grads",
    )(place, x)


def start_loads(sources, targets, sems):
    @pl.when(pl.program_id(0) == 0)
    def _():
        for n, (source, target) in enumerate(zip(sources, targets)):
            pltpu.make_async_copy(source, target, sems.at[n]).start()


def wait_load(source, target, sems, n):
    @pl.when(pl.program_id(0) == 0)
    def _():
        pltpu.make_async_copy(source, target, sems.at[n]).wait()


def column_row(extra):
    rows_n, per_row = 8, 2
    stride = extra.shape[0] // rows_n
    parts = [extra[r * stride + j : r * stride + j + 1, :] for r in range(rows_n) for j in range(per_row)]
    return jnp.concatenate(parts, axis=1)


def forward_body(x_ref, extra_ref, weights, sources, sems, outs, rc_scr):
    wg_ref, wu_ref, wd_ref = weights
    out_ref, hg_ref, g_ref, u_ref, gate_ref, rc_ref = outs
    if sources:
        start_loads(sources, weights, sems)

    @pl.when(pl.program_id(0) == 0)
    def _():
        row = column_row(extra_ref[...].astype(F32))
        rc_scr[...] = jnp.broadcast_to(row, rc_scr.shape).astype(BF16)
        rc_ref[...] = jnp.broadcast_to(row, rc_ref.shape)

    x = x_ref[...]
    gate = jax.nn.sigmoid(dot_nt(x, rc_scr[...]))
    gate_ref[...] = gate
    if sources:
        wait_load(sources[0], wg_ref, sems, 0)
    g = dot_nt(x, wg_ref[...])
    g_ref[...] = g
    if sources:
        wait_load(sources[1], wu_ref, sems, 1)
    u = dot_nt(x, wu_ref[...])
    u_ref[...] = u
    gated = (g * jax.nn.sigmoid(g) * u * gate[:, :1]).astype(BF16)
    hg_ref[...] = gated
    if sources:
        wait_load(sources[2], wd_ref, sems, 2)
    out_ref[...] = dot_nn(gated, wd_ref[...]).astype(BF16)


def forward_loading_kernel(x_ref, extra_ref, sg, su, sd, *refs):
    *outs, wg, wu, wd, rc_scr, sems = refs
    forward_body(x_ref, extra_ref, (wg, wu, wd), (sg, su, sd), sems, outs, rc_scr)


def forward_kernel(x_ref, extra_ref, wg, wu, wd, *refs):
    *outs, rc_scr = refs
    forward_body(x_ref, extra_ref, (wg, wu, wd), (), None, outs, rc_scr)


def forward(x, weights, loading):
    rows = x.shape[0]
    ff, width = weights[0].shape
    blk = 256
    row_blk = lambda n: pl.BlockSpec((blk, n), lambda i: (i, 0))
    outs = [
        jax.ShapeDtypeStruct((rows, width), BF16),
        jax.ShapeDtypeStruct((rows, ff), BF16),
        jax.ShapeDtypeStruct((rows, ff), F32),
        jax.ShapeDtypeStruct((rows, ff), F32),
        jax.ShapeDtypeStruct((rows, LANES), F32),
        jax.ShapeDtypeStruct((CAP, width), F32),
    ]
    specs = [row_blk(width), row_blk(ff), row_blk(ff), row_blk(ff), row_blk(LANES), whole((CAP, width))]
    scratch = [pltpu.VMEM((LANES, width), BF16)]
    if loading:
        outs += [pltpu.VMEM((ff, width), BF16)] * 3
        specs += [VMEM] * 3
        scratch += [pltpu.SemaphoreType.DMA((3,))]
    got = pl.pallas_call(
        forward_loading_kernel if loading else forward_kernel,
        grid=(rows // blk,),
        out_shape=tuple(outs),
        in_specs=[row_blk(width), pl.BlockSpec((rows, LANES), lambda i: (0, width // LANES))]
        + [HBM if loading else VMEM] * 3,
        out_specs=tuple(specs),
        scratch_shapes=scratch,
        compiler_params=pltpu.CompilerParams(dimension_semantics=("arbitrary",), vmem_limit_bytes=KEEPING),
        cost_estimate=cost(6 * rows * ff * width, 6 * ff * width + 8 * rows * width),
        name="expert_forward",
    )(x, x, *weights)
    return got[:6], tuple(in_vmem(w) for w in got[6:])


def backward_body(gr_ref, g_ref, u_ref, gate_ref, weights, sources, sems, outs):
    wd_ref, wg_ref, wu_ref = weights
    back_ref, dg_ref, du_ref, gg_ref = outs
    if sources:
        start_loads(sources, weights, sems)
        wait_load(sources[0], wd_ref, sems, 0)
    dh = dot_nt(gr_ref[...], wd_ref[...])
    g = g_ref[...]
    u = u_ref[...]
    s = jax.nn.sigmoid(g)
    act = g * s
    gg_ref[...] = jnp.broadcast_to(jnp.sum(dh * (act * u), axis=1, keepdims=True), gg_ref.shape)
    dh = dh * gate_ref[:, :1]
    dg = (dh * u * s * (1.0 + g * (1.0 - s))).astype(BF16)
    du = (dh * act).astype(BF16)
    dg_ref[...] = dg
    du_ref[...] = du
    if sources:
        wait_load(sources[1], wg_ref, sems, 1)
    back = dot_nn(dg, wg_ref[...])
    if sources:
        wait_load(sources[2], wu_ref, sems, 2)
    back_ref[...] = (back + dot_nn(du, wu_ref[...])).astype(BF16)


def backward_loading_kernel(gr, g, u, gate, sd, sg, su, *refs):
    *outs, wd, wg, wu, sems = refs
    backward_body(gr, g, u, gate, (wd, wg, wu), (sd, sg, su), sems, outs)


def backward_kernel(gr, g, u, gate, wd, wg, wu, *outs):
    backward_body(gr, g, u, gate, (wd, wg, wu), (), None, outs)


def backward(gr, g, u, gate, weights, loading):
    rows, width = gr.shape
    ff = weights[0].shape[0]
    blk = 256
    row_blk = lambda n: pl.BlockSpec((blk, n), lambda i: (i, 0))
    outs = [
        jax.ShapeDtypeStruct((rows, width), BF16),
        jax.ShapeDtypeStruct((rows, ff), BF16),
        jax.ShapeDtypeStruct((rows, ff), BF16),
        jax.ShapeDtypeStruct((rows, LANES), F32),
    ]
    specs = [row_blk(width), row_blk(ff), row_blk(ff), row_blk(LANES)]
    scratch = []
    if loading:
        outs += [pltpu.VMEM((ff, width), BF16)] * 3
        specs += [VMEM] * 3
        scratch += [pltpu.SemaphoreType.DMA((3,))]
    got = pl.pallas_call(
        backward_loading_kernel if loading else backward_kernel,
        grid=(rows // blk,),
        out_shape=tuple(outs),
        in_specs=[row_blk(width), row_blk(ff), row_blk(ff), row_blk(LANES)] + [HBM if loading else VMEM] * 3,
        out_specs=tuple(specs),
        scratch_shapes=scratch,
        compiler_params=pltpu.CompilerParams(dimension_semantics=("arbitrary",), vmem_limit_bytes=KEEPING),
        cost_estimate=cost(6 * rows * ff * width, 6 * ff * width + 8 * rows * width),
        name="expert_backward",
    )(gr, g, u, gate, *weights)
    return got[:4], tuple(in_vmem(w) for w in got[4:])


def join_out_kernel(mine_ref, sib_ref, out_ref):
    rows = out_ref.shape[0]
    sib = sib_ref[pl.ds(pl.multiple_of(pl.program_id(0) * rows, rows), rows), :]
    out_ref[...] = (mine_ref[...].astype(F32) + sib.astype(F32)).astype(BF16)


def join_halves(mine, sib):
    rows, width = mine.shape
    blk = pl.BlockSpec((128, width), lambda i: (i, 0))
    return pl.pallas_call(
        join_out_kernel,
        grid=(rows // 128,),
        out_shape=jax.ShapeDtypeStruct((rows, width), BF16),
        in_specs=[blk, VMEM],
        out_specs=blk,
        compiler_params=pltpu.CompilerParams(dimension_semantics=("arbitrary",), vmem_limit_bytes=KEEPING),
        cost_estimate=cost(3 * rows * width, 6 * rows * width),
        name="join_halves",
    )(mine, in_vmem(sib))


def weight_grad_kernel(d0_ref, d1_ref, x0_ref, x1_ref, out_ref):
    out_ref[...] = (dot_tn(d0_ref[...], x0_ref[...]) + dot_tn(d1_ref[...], x1_ref[...])).astype(BF16)


def weight_grad(d0, d1, x0, x1, width):
    rows, ff = d0.shape
    part = 512
    col = pl.BlockSpec((rows, part), lambda i: (0, i))
    return pl.pallas_call(
        weight_grad_kernel,
        grid=(width // part,),
        out_shape=jax.ShapeDtypeStruct((ff, width), BF16),
        in_specs=[whole((rows, ff)), whole((rows, ff)), col, col],
        out_specs=pl.BlockSpec((ff, part), lambda i: (0, i)),
        compiler_params=pltpu.CompilerParams(dimension_semantics=("arbitrary",)),
        cost_estimate=cost(4 * rows * ff * width, 4 * rows * width + 2 * ff * width),
    )(d0, d1, x0, x1)


def join_kernel(mine_ref, sib_ref, gg_ref, gg_sib_ref, gate_ref, rc_ref, x_ref, back_ref, gain_scr, router_scr):
    step = pl.program_id(0)
    chunks, _, part = gain_scr.shape
    rows = back_ref.shape[0]

    @pl.when(step < chunks)
    def _():
        c = jnp.minimum(step, chunks - 1)
        gate = gate_ref[...]
        gl = ((gg_ref[...] + gg_sib_ref[...]) * gate * (1.0 - gate)).astype(BF16).astype(F32)[:, :1]
        x = x_ref[...].astype(F32)
        sib = sib_ref[:, pl.ds(pl.multiple_of(c * part, part), part)]
        back = mine_ref[...].astype(F32) + sib.astype(F32) + gl * rc_ref[:1, :]
        back_ref[...] = back.astype(BF16)
        gain_scr[c] = jnp.sum(x * back, axis=0, keepdims=True)
        router_scr[c] = jnp.sum(x * gl, axis=0, keepdims=True)

    @pl.when(step == chunks)
    def _():
        lanes = chunks * part // CAP
        gain = jnp.concatenate([gain_scr[c] for c in range(chunks)], axis=1)
        gain = jnp.concatenate([gain[:, j * lanes : (j + 1) * lanes] for j in range(CAP)], axis=0)
        gain = jnp.broadcast_to(gain[None], (rows // CAP, CAP, lanes)).reshape(rows, lanes)
        back_ref[:, :lanes] = gain.astype(BF16)
        router = jnp.concatenate([router_scr[c] for c in range(chunks)], axis=1)
        parts = chunks * part // LANES
        router = jnp.concatenate([router[:, j * LANES : (j + 1) * LANES] for j in range(parts)], axis=0)
        per_row = parts // 8
        pick = one_hot_rows(
            rows,
            parts,
            lambda row: jnp.where(row % CAP < per_row, row // (rows // 8) * per_row + row % CAP, -1),
        )
        back_ref[:, lanes : lanes + LANES] = dot_nn(pick, router.astype(BF16)).astype(BF16)


def join_back(mine, sib, gg, gg_sib, gate, rc, x):
    rows, width = mine.shape
    part = 512
    chunks = width // part
    at = lambda i: (0, jnp.minimum(i, chunks - 1))
    col = pl.BlockSpec((rows, part), at)
    return pl.pallas_call(
        join_kernel,
        grid=(chunks + 1,),
        out_shape=jax.ShapeDtypeStruct((rows, width + width // CAP + LANES), BF16),
        in_specs=[col, VMEM] + [whole((rows, LANES))] * 3 + [pl.BlockSpec((CAP, part), at), col],
        out_specs=pl.BlockSpec((rows, part), lambda i: (0, i)),
        scratch_shapes=[pltpu.VMEM((chunks, 1, part), F32), pltpu.VMEM((chunks, 1, part), F32)],
        compiler_params=pltpu.CompilerParams(dimension_semantics=("arbitrary",), vmem_limit_bytes=KEEPING),
        cost_estimate=cost(10 * rows * width, 8 * rows * width),
        name="join_back",
    )(mine, in_vmem(sib), gg, gg_sib, gate, rc, x)


def collect_kernel(a_ref, b_ref, c_ref, out_ref):
    rows = a_ref.shape[0]
    chips = rows // CAP
    for half, ref in enumerate((a_ref, b_ref)):
        total = jnp.sum(ref[...].astype(F32).reshape(chips, CAP, LANES), axis=0)
        out_ref[:CAP, half * LANES : (half + 1) * LANES] = total
    for j in range(2):
        pick = one_hot_rows(chips, rows, lambda row: row * CAP + j)
        out_ref[CAP:, j * LANES : (j + 1) * LANES] = dot_nn(pick, c_ref[...])


def collect(rows_in, width):
    rows = rows_in.shape[0]
    first = width // LANES
    lane = lambda k: pl.BlockSpec((rows, LANES), lambda i: (0, first + k))
    return pl.pallas_call(
        collect_kernel,
        grid=(1,),
        out_shape=jax.ShapeDtypeStruct((CAP + rows // CAP, 2 * LANES), F32),
        in_specs=[lane(0), lane(1), lane(2)],
        out_specs=whole((CAP + rows // CAP, 2 * LANES)),
        compiler_params=pltpu.CompilerParams(vmem_limit_bytes=KEEPING),
        cost_estimate=cost(rows * rows * LANES, 6 * rows * LANES),
        name="collect_sums",
    )(rows_in, rows_in, rows_in)


def mix_kernel(place_ref, rows_ref, tok_ref, mixed_ref, acc_ref):
    step = pl.program_id(0)
    part = dot_tn(place_ref[...], rows_ref[...])

    @pl.when(step == 0)
    def _():
        acc_ref[...] = part

    @pl.when(step > 0)
    def _():
        acc_ref[...] += part

    @pl.when(step == pl.num_programs(0) - 1)
    def _():
        mixed_ref[...] = (tok_ref[...].astype(F32) + acc_ref[...]).astype(BF16)


def mix(place, rows, tokens):
    slots, tok_count = place.shape
    width = tokens.shape[1]
    part = 128
    return pl.pallas_call(
        mix_kernel,
        grid=(slots // part,),
        out_shape=jax.ShapeDtypeStruct((tok_count, width), BF16),
        in_specs=[
            pl.BlockSpec((part, tok_count), lambda i: (i, 0)),
            pl.BlockSpec((part, width), lambda i: (i, 0)),
            whole((tok_count, width)),
        ],
        out_specs=whole((tok_count, width)),
        scratch_shapes=[pltpu.VMEM((tok_count, width), F32)],
        compiler_params=pltpu.CompilerParams(dimension_semantics=("arbitrary",)),
        cost_estimate=cost(2 * slots * tok_count * width, 2 * slots * width),
        name="mix_outputs",
    )(place, rows, tokens)


def finish_kernel(place_ref, rows_ref, tok_ref, gain_ref, up_ref, out_ref, acc_ref):
    step = pl.program_id(0)
    part = dot_tn(place_ref[...], rows_ref[...])

    @pl.when(step == 0)
    def _():
        acc_ref[...] = part

    @pl.when(step > 0)
    def _():
        acc_ref[...] += part

    @pl.when(step == pl.num_programs(0) - 1)
    def _():
        x = tok_ref[...].astype(F32)
        inverse = lax.rsqrt(jnp.mean(x * x, axis=1, keepdims=True) + EPSILON)
        normed = x * inverse
        gn = acc_ref[...] * gain_ref[...]
        out = up_ref[...].astype(F32) + inverse * (gn - normed * jnp.mean(gn * normed, axis=1, keepdims=True))
        out_ref[...] = out.astype(BF16)


def finish(place, rows, tokens, gain, upstream):
    slots, tok_count = place.shape
    width = tokens.shape[1]
    part = 128
    return pl.pallas_call(
        finish_kernel,
        grid=(slots // part,),
        out_shape=jax.ShapeDtypeStruct((tok_count, width), BF16),
        in_specs=[
            pl.BlockSpec((part, tok_count), lambda i: (i, 0)),
            pl.BlockSpec((part, width), lambda i: (i, 0)),
            whole((tok_count, width)),
            whole((1, width)),
            whole((tok_count, width)),
        ],
        out_specs=whole((tok_count, width)),
        scratch_shapes=[pltpu.VMEM((tok_count, width), F32)],
        compiler_params=pltpu.CompilerParams(dimension_semantics=("arbitrary",), vmem_limit_bytes=KEEPING),
        cost_estimate=cost(2 * slots * tok_count * width, 2 * slots * width),
        name="finish_tokens",
    )(place, rows, tokens, gain, upstream)


def across(block, axis, bit):
    count = lax.axis_size(axis)
    return lax.ppermute(block, axis, [(i, i ^ bit) for i in range(count)])


def exchange(x, experts):
    rows, width = x.shape
    return lax.all_to_all(x.reshape(experts, -1, width), CHIPS, 0, 0, tiled=True).reshape(rows, width)


def local(tokens, norm_gain, router_weight, expert_ids, w_gate, w_up, w_down, grad_mixed):
    _, width = tokens.shape
    experts = router_weight.shape[1]
    slots = experts * CAP
    gain = norm_gain.reshape(1, width)
    wg, wu, wd = w_gate[0].T, w_up[0].T, w_down[0]

    send_in, place = dispatch(tokens, gain, expert_ids.T, router_weight.T, slots)
    in_0 = in_hbm(exchange(send_in, experts))
    send_grad = place_rows(place, grad_mixed)
    gr_0 = in_hbm(exchange(send_grad, experts))
    in_1 = across(in_0, CORE, 1)
    gr_1 = across(gr_0, CORE, 1)

    (out_1, hg_1, g_1, u_1, gate_1, _), near = forward(in_1, (wg, wu, wd), True)
    (out_0, hg_0, g_0, u_0, gate_0, rc), _ = forward(in_0, near, False)
    out_s = across(out_1, CORE, 1)
    out = join_halves(out_0, out_s)
    got_out = in_hbm(exchange(out, experts))
    mixed = mix(place, got_out, tokens)

    (back_1, dg_1, du_1, gg_1), near = backward(gr_1, g_1, u_1, gate_1, (wd, wg, wu), True)
    (back_0, dg_0, du_0, gg_0), _ = backward(gr_0, g_0, u_0, gate_0, near, False)
    back_s = across(back_1, CORE, 1)
    gg_s = across(gg_1, CORE, 1)
    back = join_back(back_0, back_s, gg_0, gg_s, gate_0, rc, in_0)
    got_back = exchange(back, experts)
    grad_tokens = finish(place, got_back, tokens, gain, grad_mixed)

    grad_down = weight_grad(hg_0, hg_1, gr_0, gr_1, width)
    grad_gate = weight_grad(dg_0, dg_1, in_0, in_1, width)
    grad_up = weight_grad(du_0, du_1, in_0, in_1, width)

    sums = collect(got_back, width)
    sums = sums + across(sums, CORE, 1)
    grad_gain = sums[:CAP].reshape(width) / norm_gain
    grad_router = sums[CAP:].T
    return (
        mixed,
        grad_tokens,
        grad_gain,
        grad_router,
        grad_gate.T[None],
        grad_up.T[None],
        grad_down[None],
    )


def solution(mesh):
    finer = Mesh(mesh.devices.reshape(4, 2, 2, 4, 2), ROW_COL)
    placed = (
        P(ROW_COL, None),
        P(),
        P(ROW, None),
        P(ROW_COL, None),
        P(ROW_COL, None, None),
        P(ROW_COL, None, None),
        P(ROW_COL, None, None),
        P(ROW_COL, None),
    )
    return jax.shard_map(
        local,
        mesh=finer,
        in_specs=placed,
        out_specs=(
            P(ROW_COL, None),
            P(ROW_COL, None),
            P(),
            P(ROW, None),
            P(ROW_COL, None, None),
            P(ROW_COL, None, None),
            P(ROW_COL, None, None),
        ),
        check_vma=False,
    )
```

```python
import jax
import jax.numpy as jnp
from jax import lax
from jax.experimental import pallas as pl
from jax.experimental.pallas import tpu as pltpu
from jax.sharding import Mesh
from jax.sharding import PartitionSpec as P


ROW_COL = ("row_0", "row_1", "col_0", "col_1", "col_2")
CHIPS = ("row_0", "row_1", "col_0", "col_1")
ROW = ("row_0", "row_1")
CORE = "col_2"
CAP = 8
LANES = 128
F32 = jnp.float32
BF16 = jnp.bfloat16
EPSILON = 1e-06
KEEPING = 51 << 20


def dot_nn(a, b):
    return lax.dot_general(a, b, (((1,), (0,)), ((), ())), preferred_element_type=F32)


def dot_nt(a, b):
    return lax.dot_general(a, b, (((1,), (1,)), ((), ())), preferred_element_type=F32)


def dot_tn(a, b):
    return lax.dot_general(a, b, (((0,), (0,)), ((), ())), preferred_element_type=F32)


VMEM = pl.BlockSpec(memory_space=pltpu.VMEM)
HBM = pl.BlockSpec(memory_space=pltpu.HBM)


def in_vmem(x):
    return pltpu.with_memory_space_constraint(x, pltpu.VMEM)


def in_hbm(x):
    return pltpu.with_memory_space_constraint(x, pltpu.HBM)


def cost(flops, bytes_accessed):
    return pl.CostEstimate(flops=int(flops), bytes_accessed=int(bytes_accessed), transcendentals=0)


def whole(shape):
    return pl.BlockSpec(shape, lambda i: (0,) * len(shape))


def one_hot_rows(rows, cols, column_of):
    row = lax.broadcasted_iota(jnp.int32, (rows, cols), 0)
    col = lax.broadcasted_iota(jnp.int32, (rows, cols), 1)
    return jnp.where(column_of(row) == col, 1.0, 0.0).astype(BF16)


def dispatch_kernel(tok_ref, gain_ref, ids_ref, router_ref, send_ref, place_ref, scaled_scr):
    step = pl.program_id(0)
    chunks, tok_count, width = scaled_scr.shape
    slots = place_ref.shape[0]
    experts = slots // CAP

    @pl.when(step == 0)
    def _():
        x = tok_ref[...].astype(F32)
        inverse = lax.rsqrt(jnp.mean(x * x, axis=1, keepdims=True) + EPSILON)
        scaled = (x * inverse * gain_ref[...]).astype(BF16)
        for c in range(chunks):
            scaled_scr[c] = scaled[:, c * width : (c + 1) * width]
        ids = ids_ref[...]
        expert = lax.broadcasted_iota(jnp.int32, (experts, tok_count), 0)
        named = jnp.zeros((experts, tok_count), F32)
        for k in range(ids.shape[0]):
            named = named + jnp.where(ids[k : k + 1, :] == expert, 1.0, 0.0)
        before = lax.broadcasted_iota(jnp.int32, (tok_count, tok_count), 0)
        after = lax.broadcasted_iota(jnp.int32, (tok_count, tok_count), 1)
        earlier = jnp.where(before < after, 1.0, 0.0).astype(BF16)
        rank = dot_nn(named.astype(BF16), earlier)
        order = (named * (rank + 1.0)).astype(BF16)
        order_of = dot_nn(one_hot_rows(slots, experts, lambda row: row // CAP), order)
        want = (lax.broadcasted_iota(jnp.int32, (slots, tok_count), 0) % CAP + 1).astype(F32)
        place_ref[...] = jnp.where(order_of == want, 1.0, 0.0).astype(BF16)

    @pl.when(step < chunks)
    def _():
        send_ref[...] = dot_nn(place_ref[...], scaled_scr[jnp.minimum(step, chunks - 1)]).astype(BF16)

    @pl.when(step == chunks)
    def _():
        extra = jnp.zeros((slots, LANES), F32)
        for j in range(router_ref.shape[1] // LANES):
            pick = one_hot_rows(slots, experts, lambda row: jnp.where(row % CAP == j, row // CAP, -1))
            extra = extra + dot_nn(pick, router_ref[:, j * LANES : (j + 1) * LANES])
        send_ref[:, :LANES] = extra.astype(BF16)


def dispatch(tokens, gain, ids, router, slots):
    tok_count, width = tokens.shape
    chunks = 4
    part = width // chunks
    return pl.pallas_call(
        dispatch_kernel,
        grid=(chunks + 1,),
        out_shape=(
            jax.ShapeDtypeStruct((slots, width + LANES), BF16),
            jax.ShapeDtypeStruct((slots, tok_count), BF16),
        ),
        in_specs=[whole((tok_count, width)), whole((1, width)), whole(ids.shape), whole(router.shape)],
        out_specs=(
            pl.BlockSpec((slots, part), lambda i: (0, i)),
            whole((slots, tok_count)),
        ),
        scratch_shapes=[pltpu.VMEM((chunks, tok_count, part), BF16)],
        compiler_params=pltpu.CompilerParams(dimension_semantics=("arbitrary",)),
        cost_estimate=cost(2 * slots * tok_count * width, 2 * slots * width * 2),
        name="dispatch_tokens",
    )(tokens, gain, ids, router)


def place_kernel(place_ref, x_ref, send_ref):
    send_ref[...] = dot_nn(place_ref[...], x_ref[...]).astype(BF16)


def place_rows(place, x):
    slots, tok_count = place.shape
    width = x.shape[1]
    chunks = 4
    part = width // chunks
    return pl.pallas_call(
        place_kernel,
        grid=(chunks,),
        out_shape=jax.ShapeDtypeStruct((slots, width), BF16),
        in_specs=[whole((slots, tok_count)), pl.BlockSpec((tok_count, part), lambda i: (0, i))],
        out_specs=pl.BlockSpec((slots, part), lambda i: (0, i)),
        compiler_params=pltpu.CompilerParams(dimension_semantics=("arbitrary",)),
        cost_estimate=cost(2 * slots * tok_count * width, 2 * slots * width * 2),
        name="dispatch_grads",
    )(place, x)


CHUNKS = 4


class Copies:
    def __init__(self, sems):
        self.sems = sems
        self.started = []

    def start(self, source, target):
        copy = pltpu.make_async_copy(source, target, self.sems.at[len(self.started)])
        copy.start()
        self.started.append(copy)
        return copy


def column_row(extra):
    rows_n, per_row = 8, 2
    stride = extra.shape[0] // rows_n
    parts = [extra[r * stride + j : r * stride + j + 1, :] for r in range(rows_n) for j in range(per_row)]
    return jnp.concatenate(parts, axis=1)


def forward_body(x_hbm, weights, sources, outs, scratch):
    wg, wu, wd = weights
    out_hbm, hg_hbm, fg_hbm, fu_hbm, gate_ref, rc_ref = outs
    block, hg, fg, fu, sems = scratch
    width = wd.shape[1]
    copies = Copies(sems)
    x, out = (x_hbm, block) if sources else (block, out_hbm)
    if not sources:
        copies.start(x_hbm, x).wait()
    got_w = [copies.start(source, target) for source, target in zip(sources, weights)]
    waits = lambda n: got_w[n].wait() if got_w else None
    rows = x[:, :width]
    row = column_row(x[:, width:].astype(F32))
    rc_ref[...] = jnp.broadcast_to(row, rc_ref.shape)
    gate = jax.nn.sigmoid(dot_nt(rows, jnp.broadcast_to(row, (LANES, width)).astype(BF16)))
    gate_ref[...] = gate
    gate = gate[:, :1]
    waits(0)
    g = dot_nt(rows, wg[...])
    waits(1)
    u = dot_nt(rows, wu[...])
    s = jax.nn.sigmoid(g)
    act = gate * (g * s)
    hg[...] = (act * u).astype(BF16)
    fu[...] = act.astype(BF16)
    fg[...] = (gate * s * u * (1.0 + g * (1.0 - s))).astype(BF16)
    puts = [copies.start(hg, hg_hbm), copies.start(fg, fg_hbm), copies.start(fu, fu_hbm)]
    waits(2)
    part = width // CHUNKS
    for c in range(CHUNKS):
        cols = slice(c * part, (c + 1) * part)
        out[:, cols] = dot_nn(hg[...], wd[:, cols]).astype(BF16)
        if sources:
            puts.append(copies.start(out.at[:, cols], out_hbm.at[:, cols]))
    for put in puts:
        put.wait()


def forward_loading_kernel(x_hbm, sg, su, sd, *refs):
    forward_body(x_hbm, refs[6:9], (sg, su, sd), refs[:6], refs[9:])


def forward_kernel(x_hbm, wg, wu, wd, *refs):
    forward_body(x_hbm, (wg, wu, wd), (), refs[:6], refs[6:])


def forward(x, weights, loading):
    rows = x.shape[0]
    ff, width = weights[0].shape
    outs = [
        jax.ShapeDtypeStruct((rows, width), BF16) if loading else pltpu.VMEM((rows, width), BF16),
        jax.ShapeDtypeStruct((rows, ff), BF16),
        jax.ShapeDtypeStruct((rows, ff), BF16),
        jax.ShapeDtypeStruct((rows, ff), BF16),
        jax.ShapeDtypeStruct((rows, LANES), F32),
        jax.ShapeDtypeStruct((CAP, width), F32),
    ]
    specs = [HBM if loading else VMEM] + [HBM] * 3 + [whole((rows, LANES)), whole((CAP, width))]
    if loading:
        outs += [pltpu.VMEM((ff, width), BF16)] * 3
        specs += [VMEM] * 3
    got = pl.pallas_call(
        forward_loading_kernel if loading else forward_kernel,
        grid=(1,),
        out_shape=tuple(outs),
        in_specs=[VMEM if loading else HBM] + [HBM if loading else VMEM] * 3,
        out_specs=tuple(specs),
        scratch_shapes=[
            pltpu.VMEM((rows, width) if loading else x.shape, BF16),
            pltpu.VMEM((rows, ff), BF16),
            pltpu.VMEM((rows, ff), BF16),
            pltpu.VMEM((rows, ff), BF16),
            pltpu.SemaphoreType.DMA((7 + CHUNKS,)),
        ],
        compiler_params=pltpu.CompilerParams(dimension_semantics=("arbitrary",), vmem_limit_bytes=KEEPING),
        cost_estimate=cost(6 * rows * ff * width, 6 * ff * width + 8 * rows * width),
        name="expert_forward",
    )(in_vmem(x) if loading else x, *weights)
    return got[:6], tuple(in_vmem(w) for w in got[6:])


def backward_body(ins, weights, sources, outs, scratch):
    wd, wg, wu = weights
    back_hbm, dg_hbm, du_hbm, gg_ref = outs
    block, hg, fg, fu, dg, du, sems = scratch
    width = wd.shape[1]
    copies = Copies(sems)
    gr, back = (ins[0], block) if sources else (block, back_hbm)
    got = [] if sources else [copies.start(ins[0], gr)]
    got_w = [copies.start(source, target) for source, target in zip(sources[:1], weights[:1])]
    got_more = [copies.start(source, target) for source, target in zip(ins[1:], (hg, fg, fu))]
    got_w += [copies.start(source, target) for source, target in zip(sources[1:], weights[1:])]
    waits = lambda n: got_w[n].wait() if got_w else None
    for copy in got:
        copy.wait()
    waits(0)
    dh = dot_nt(gr[...], wd[...])
    for copy in got_more:
        copy.wait()
    inner = jnp.sum(dh * hg[...].astype(F32), axis=1, keepdims=True)
    gg_ref[...] = jnp.broadcast_to(inner, gg_ref.shape)
    dg[...] = (dh * fg[...].astype(F32)).astype(BF16)
    du[...] = (dh * fu[...].astype(F32)).astype(BF16)
    puts = [copies.start(dg, dg_hbm), copies.start(du, du_hbm)]
    waits(1)
    waits(2)
    part = width // CHUNKS
    for c in range(CHUNKS):
        cols = slice(c * part, (c + 1) * part)
        back[:, cols] = (dot_nn(dg[...], wg[:, cols]) + dot_nn(du[...], wu[:, cols])).astype(BF16)
        if sources:
            puts.append(copies.start(back.at[:, cols], back_hbm.at[:, cols]))
    for put in puts:
        put.wait()


def backward_loading_kernel(gr, hg, fg, fu, sd, sg, su, *refs):
    backward_body((gr, hg, fg, fu), refs[4:7], (sd, sg, su), refs[:4], refs[7:])


def backward_kernel(gr, hg, fg, fu, wd, wg, wu, *refs):
    backward_body((gr, hg, fg, fu), (wd, wg, wu), (), refs[:4], refs[4:])


def backward(gr, hg, fg, fu, weights, loading):
    rows, width = gr.shape
    ff = weights[0].shape[0]
    outs = [
        jax.ShapeDtypeStruct((rows, width), BF16) if loading else pltpu.VMEM((rows, width), BF16),
        jax.ShapeDtypeStruct((rows, ff), BF16),
        jax.ShapeDtypeStruct((rows, ff), BF16),
        jax.ShapeDtypeStruct((rows, LANES), F32),
    ]
    specs = [HBM if loading else VMEM] + [HBM] * 2 + [whole((rows, LANES))]
    if loading:
        outs += [pltpu.VMEM((ff, width), BF16)] * 3
        specs += [VMEM] * 3
    got = pl.pallas_call(
        backward_loading_kernel if loading else backward_kernel,
        grid=(1,),
        out_shape=tuple(outs),
        in_specs=[VMEM if loading else HBM] + [HBM] * 3 + [HBM if loading else VMEM] * 3,
        out_specs=tuple(specs),
        scratch_shapes=[pltpu.VMEM((rows, width), BF16)]
        + [pltpu.VMEM((rows, ff), BF16)] * 3
        + [pltpu.VMEM((rows, ff), BF16)] * 2
        + [pltpu.SemaphoreType.DMA((9 + CHUNKS,))],
        compiler_params=pltpu.CompilerParams(dimension_semantics=("arbitrary",), vmem_limit_bytes=KEEPING),
        cost_estimate=cost(6 * rows * ff * width, 6 * ff * width + 8 * rows * width),
        name="expert_backward",
    )(in_vmem(gr) if loading else gr, hg, fg, fu, *weights)
    return got[:4], tuple(in_vmem(w) for w in got[4:])


def join_out_kernel(mine_ref, sib_ref, out_ref):
    rows = out_ref.shape[0]
    here = pl.ds(pl.multiple_of(pl.program_id(0) * rows, rows), rows)
    out_ref[...] = (mine_ref[here, :].astype(F32) + sib_ref[here, :].astype(F32)).astype(BF16)


def join_halves(mine, sib):
    rows, width = mine.shape
    blk = pl.BlockSpec((128, width), lambda i: (i, 0))
    return pl.pallas_call(
        join_out_kernel,
        grid=(rows // 128,),
        out_shape=jax.ShapeDtypeStruct((rows, width), BF16),
        in_specs=[VMEM, VMEM],
        out_specs=blk,
        compiler_params=pltpu.CompilerParams(dimension_semantics=("arbitrary",), vmem_limit_bytes=KEEPING),
        cost_estimate=cost(3 * rows * width, 6 * rows * width),
        name="join_halves",
    )(in_vmem(mine), in_vmem(sib))


def weight_grad_kernel(d0_ref, d1_ref, x0_ref, x1_ref, out_ref):
    out_ref[...] = (dot_tn(d0_ref[...], x0_ref[...]) + dot_tn(d1_ref[...], x1_ref[...])).astype(BF16)


def weight_grad(d0, d1, x0, x1, width):
    rows, ff = d0.shape
    part = 512
    col = pl.BlockSpec((rows, part), lambda i: (0, i))
    return pl.pallas_call(
        weight_grad_kernel,
        grid=(width // part,),
        out_shape=jax.ShapeDtypeStruct((ff, width), BF16),
        in_specs=[whole((rows, ff)), whole((rows, ff)), col, col],
        out_specs=pl.BlockSpec((ff, part), lambda i: (0, i)),
        compiler_params=pltpu.CompilerParams(dimension_semantics=("arbitrary",)),
        cost_estimate=cost(4 * rows * ff * width, 4 * rows * width + 2 * ff * width),
    )(d0, d1, x0, x1)


def join_kernel(mine_ref, sib_ref, gg_ref, gg_sib_ref, gate_ref, rc_ref, x_ref, back_ref, gain_scr, router_scr):
    step = pl.program_id(0)
    chunks, _, part = gain_scr.shape
    rows = back_ref.shape[0]

    @pl.when(step < chunks)
    def _():
        c = jnp.minimum(step, chunks - 1)
        gate = gate_ref[...]
        gl = ((gg_ref[...] + gg_sib_ref[...]) * (1.0 - gate)).astype(BF16).astype(F32)[:, :1]
        x = x_ref[...].astype(F32)
        here = pl.ds(pl.multiple_of(c * part, part), part)
        back = mine_ref[:, here].astype(F32) + sib_ref[:, here].astype(F32) + gl * rc_ref[:1, :]
        back_ref[...] = back.astype(BF16)
        gain_scr[c] = jnp.sum(x * back, axis=0, keepdims=True)
        router_scr[c] = jnp.sum(x * gl, axis=0, keepdims=True)

    @pl.when(step == chunks)
    def _():
        lanes = chunks * part // CAP
        gain = jnp.concatenate([gain_scr[c] for c in range(chunks)], axis=1)
        gain = jnp.concatenate([gain[:, j * lanes : (j + 1) * lanes] for j in range(CAP)], axis=0)
        gain = jnp.broadcast_to(gain[None], (rows // CAP, CAP, lanes)).reshape(rows, lanes)
        back_ref[:, :lanes] = gain.astype(BF16)
        router = jnp.concatenate([router_scr[c] for c in range(chunks)], axis=1)
        parts = chunks * part // LANES
        router = jnp.concatenate([router[:, j * LANES : (j + 1) * LANES] for j in range(parts)], axis=0)
        per_row = parts // 8
        pick = one_hot_rows(
            rows,
            parts,
            lambda row: jnp.where(row % CAP < per_row, row // (rows // 8) * per_row + row % CAP, -1),
        )
        back_ref[:, lanes : lanes + LANES] = dot_nn(pick, router.astype(BF16)).astype(BF16)


def join_back(mine, sib, gg, gg_sib, gate, rc, x):
    rows, width = mine.shape
    part = 512
    chunks = width // part
    at = lambda i: (0, jnp.minimum(i, chunks - 1))
    col = pl.BlockSpec((rows, part), at)
    return pl.pallas_call(
        join_kernel,
        grid=(chunks + 1,),
        out_shape=jax.ShapeDtypeStruct((rows, width + width // CAP + LANES), BF16),
        in_specs=[VMEM, VMEM] + [whole((rows, LANES))] * 3 + [pl.BlockSpec((CAP, part), at), col],
        out_specs=pl.BlockSpec((rows, part), lambda i: (0, i)),
        scratch_shapes=[pltpu.VMEM((chunks, 1, part), F32), pltpu.VMEM((chunks, 1, part), F32)],
        compiler_params=pltpu.CompilerParams(dimension_semantics=("arbitrary",), vmem_limit_bytes=KEEPING),
        cost_estimate=cost(10 * rows * width, 8 * rows * width),
        name="join_back",
    )(in_vmem(mine), in_vmem(sib), gg, gg_sib, gate, rc, x)


def collect_kernel(a_ref, b_ref, c_ref, out_ref):
    rows = a_ref.shape[0]
    chips = rows // CAP
    for half, ref in enumerate((a_ref, b_ref)):
        total = jnp.sum(ref[...].astype(F32).reshape(chips, CAP, LANES), axis=0)
        out_ref[:CAP, half * LANES : (half + 1) * LANES] = total
    for j in range(2):
        pick = one_hot_rows(chips, rows, lambda row: row * CAP + j)
        out_ref[CAP:, j * LANES : (j + 1) * LANES] = dot_nn(pick, c_ref[...])


def collect(rows_in, width):
    rows = rows_in.shape[0]
    first = width // LANES
    lane = lambda k: pl.BlockSpec((rows, LANES), lambda i: (0, first + k))
    return pl.pallas_call(
        collect_kernel,
        grid=(1,),
        out_shape=jax.ShapeDtypeStruct((CAP + rows // CAP, 2 * LANES), F32),
        in_specs=[lane(0), lane(1), lane(2)],
        out_specs=whole((CAP + rows // CAP, 2 * LANES)),
        compiler_params=pltpu.CompilerParams(vmem_limit_bytes=50 << 20),
        cost_estimate=cost(rows * rows * LANES, 6 * rows * LANES),
        name="collect_sums",
    )(rows_in, rows_in, rows_in)


def mix_kernel(place_ref, rows_ref, tok_ref, mixed_ref, acc_ref):
    step = pl.program_id(0)
    part = dot_tn(place_ref[...], rows_ref[...])

    @pl.when(step == 0)
    def _():
        acc_ref[...] = part

    @pl.when(step > 0)
    def _():
        acc_ref[...] += part

    @pl.when(step == pl.num_programs(0) - 1)
    def _():
        mixed_ref[...] = (tok_ref[...].astype(F32) + acc_ref[...]).astype(BF16)


def mix(place, rows, tokens):
    slots, tok_count = place.shape
    width = tokens.shape[1]
    part = 128
    return pl.pallas_call(
        mix_kernel,
        grid=(slots // part,),
        out_shape=jax.ShapeDtypeStruct((tok_count, width), BF16),
        in_specs=[
            pl.BlockSpec((part, tok_count), lambda i: (i, 0)),
            pl.BlockSpec((part, width), lambda i: (i, 0)),
            whole((tok_count, width)),
        ],
        out_specs=whole((tok_count, width)),
        scratch_shapes=[pltpu.VMEM((tok_count, width), F32)],
        compiler_params=pltpu.CompilerParams(dimension_semantics=("arbitrary",)),
        cost_estimate=cost(2 * slots * tok_count * width, 2 * slots * width),
        name="mix_outputs",
    )(place, rows, tokens)


def finish_kernel(place_ref, rows_ref, tok_ref, gain_ref, up_ref, out_ref, acc_ref):
    step = pl.program_id(0)
    part = dot_tn(place_ref[...], rows_ref[...])

    @pl.when(step == 0)
    def _():
        acc_ref[...] = part

    @pl.when(step > 0)
    def _():
        acc_ref[...] += part

    @pl.when(step == pl.num_programs(0) - 1)
    def _():
        x = tok_ref[...].astype(F32)
        inverse = lax.rsqrt(jnp.mean(x * x, axis=1, keepdims=True) + EPSILON)
        normed = x * inverse
        gn = acc_ref[...] * gain_ref[...]
        out = up_ref[...].astype(F32) + inverse * (gn - normed * jnp.mean(gn * normed, axis=1, keepdims=True))
        out_ref[...] = out.astype(BF16)


def finish(place, rows, tokens, gain, upstream):
    slots, tok_count = place.shape
    width = tokens.shape[1]
    part = 128
    return pl.pallas_call(
        finish_kernel,
        grid=(slots // part,),
        out_shape=jax.ShapeDtypeStruct((tok_count, width), BF16),
        in_specs=[
            pl.BlockSpec((part, tok_count), lambda i: (i, 0)),
            pl.BlockSpec((part, width), lambda i: (i, 0)),
            whole((tok_count, width)),
            whole((1, width)),
            whole((tok_count, width)),
        ],
        out_specs=whole((tok_count, width)),
        scratch_shapes=[pltpu.VMEM((tok_count, width), F32)],
        compiler_params=pltpu.CompilerParams(dimension_semantics=("arbitrary",), vmem_limit_bytes=50 << 20),
        cost_estimate=cost(2 * slots * tok_count * width, 2 * slots * width),
        name="finish_tokens",
    )(place, rows, tokens, gain, upstream)


def across(block, axis, bit):
    count = lax.axis_size(axis)
    return lax.ppermute(block, axis, [(i, i ^ bit) for i in range(count)])


def exchange(x, experts):
    rows, width = x.shape
    return lax.all_to_all(x.reshape(experts, -1, width), CHIPS, 0, 0, tiled=True).reshape(rows, width)


def local(tokens, norm_gain, router_weight, expert_ids, w_gate, w_up, w_down, grad_mixed):
    _, width = tokens.shape
    experts = router_weight.shape[1]
    slots = experts * CAP
    gain = norm_gain.reshape(1, width)
    wg, wu, wd = w_gate[0].T, w_up[0].T, w_down[0]

    send_in, place = dispatch(tokens, gain, expert_ids.T, router_weight.T, slots)
    in_0 = in_hbm(exchange(send_in, experts))
    send_grad = place_rows(place, grad_mixed)
    gr_0 = in_hbm(exchange(send_grad, experts))
    in_1 = across(in_0, CORE, 1)
    gr_1 = across(gr_0, CORE, 1)

    (out_1, hg_1, fg_1, fu_1, _, _), near = forward(in_1, (wg, wu, wd), True)
    (out_0, hg_0, fg_0, fu_0, gate_0, rc), _ = forward(in_0, near, False)
    out_s = across(out_1, CORE, 1)
    out = join_halves(out_0, out_s)
    got_out = in_hbm(exchange(out, experts))
    mixed = mix(place, got_out, tokens)

    (back_1, dg_1, du_1, gg_1), near = backward(gr_1, hg_1, fg_1, fu_1, (wd, wg, wu), True)
    (back_0, dg_0, du_0, gg_0), _ = backward(gr_0, hg_0, fg_0, fu_0, near, False)
    back_s = across(back_1, CORE, 1)
    gg_s = across(gg_1, CORE, 1)
    back = join_back(back_0, back_s, gg_0, gg_s, gate_0, rc, in_0)
    got_back = exchange(back, experts)
    grad_tokens = finish(place, got_back, tokens, gain, grad_mixed)

    grad_down = weight_grad(hg_0, hg_1, gr_0, gr_1, width)
    grad_gate = weight_grad(dg_0, dg_1, in_0, in_1, width)
    grad_up = weight_grad(du_0, du_1, in_0, in_1, width)

    sums = collect(got_back, width)
    sums = sums + across(sums, CORE, 1)
    grad_gain = sums[:CAP].reshape(width) / norm_gain
    grad_router = sums[CAP:].T
    return (
        mixed,
        grad_tokens,
        grad_gain,
        grad_router,
        grad_gate.T[None],
        grad_up.T[None],
        grad_down[None],
    )


def solution(mesh):
    finer = Mesh(mesh.devices.reshape(4, 2, 2, 4, 2), ROW_COL)
    placed = (
        P(ROW_COL, None),
        P(),
        P(ROW, None),
        P(ROW_COL, None),
        P(ROW_COL, None, None),
        P(ROW_COL, None, None),
        P(ROW_COL, None, None),
        P(ROW_COL, None),
    )
    return jax.shard_map(
        local,
        mesh=finer,
        in_specs=placed,
        out_specs=(
            P(ROW_COL, None),
            P(ROW_COL, None),
            P(),
            P(ROW, None),
            P(ROW_COL, None, None),
            P(ROW_COL, None, None),
            P(ROW_COL, None, None),
        ),
        check_vma=False,
    )
```

```python
import jax
import jax.numpy as jnp
from jax import lax
from jax.experimental import pallas as pl
from jax.experimental.pallas import tpu as pltpu
from jax.sharding import Mesh
from jax.sharding import PartitionSpec as P


ROW_COL = ("row_0", "row_1", "col_0", "col_1", "col_2")
CHIPS = ("row_0", "row_1", "col_0", "col_1")
ROW = ("row_0", "row_1")
CORE = "col_2"
CAP = 8
LANES = 128
F32 = jnp.float32
BF16 = jnp.bfloat16
EPSILON = 1e-06
KEEPING = 51 << 20


def dot_nn(a, b):
    return lax.dot_general(a, b, (((1,), (0,)), ((), ())), preferred_element_type=F32)


def dot_nt(a, b):
    return lax.dot_general(a, b, (((1,), (1,)), ((), ())), preferred_element_type=F32)


def dot_tn(a, b):
    return lax.dot_general(a, b, (((0,), (0,)), ((), ())), preferred_element_type=F32)


VMEM = pl.BlockSpec(memory_space=pltpu.VMEM)
HBM = pl.BlockSpec(memory_space=pltpu.HBM)


def in_vmem(x):
    return pltpu.with_memory_space_constraint(x, pltpu.VMEM)


def in_hbm(x):
    return pltpu.with_memory_space_constraint(x, pltpu.HBM)


def cost(flops, bytes_accessed):
    return pl.CostEstimate(flops=int(flops), bytes_accessed=int(bytes_accessed), transcendentals=0)


def whole(shape):
    return pl.BlockSpec(shape, lambda i: (0,) * len(shape))


def one_hot_rows(rows, cols, column_of):
    row = lax.broadcasted_iota(jnp.int32, (rows, cols), 0)
    col = lax.broadcasted_iota(jnp.int32, (rows, cols), 1)
    return jnp.where(column_of(row) == col, 1.0, 0.0).astype(BF16)


def dispatch_kernel(tok_ref, gain_ref, ids_ref, router_ref, send_hbm, place_ref, send, sems):
    tok_count, width = tok_ref.shape
    slots = place_ref.shape[0]
    experts = slots // CAP
    puts = []

    def put(lo, hi):
        copy = pltpu.make_async_copy(send.at[:, lo:hi], send_hbm.at[:, lo:hi], sems.at[len(puts)])
        copy.start()
        puts.append(copy)

    ids = ids_ref[...]
    expert = lax.broadcasted_iota(jnp.int32, (experts, tok_count), 0)
    named = jnp.zeros((experts, tok_count), F32)
    for k in range(ids.shape[0]):
        named = named + jnp.where(ids[k : k + 1, :] == expert, 1.0, 0.0)
    before = lax.broadcasted_iota(jnp.int32, (tok_count, tok_count), 0)
    after = lax.broadcasted_iota(jnp.int32, (tok_count, tok_count), 1)
    earlier = jnp.where(before < after, 1.0, 0.0).astype(BF16)
    rank = dot_nn(named.astype(BF16), earlier)
    order = (named * (rank + 1.0)).astype(BF16)
    order_of = dot_nn(one_hot_rows(slots, experts, lambda row: row // CAP), order)
    want = (lax.broadcasted_iota(jnp.int32, (slots, tok_count), 0) % CAP + 1).astype(F32)
    place = jnp.where(order_of == want, 1.0, 0.0).astype(BF16)
    place_ref[...] = place
    extra = jnp.zeros((slots, LANES), F32)
    for j in range(router_ref.shape[1] // LANES):
        pick = one_hot_rows(slots, experts, lambda row: jnp.where(row % CAP == j, row // CAP, -1))
        extra = extra + dot_nn(pick, router_ref[:, j * LANES : (j + 1) * LANES])
    send[:, width:] = extra.astype(BF16)
    put(width, width + LANES)
    x = tok_ref[...].astype(F32)
    inverse = lax.rsqrt(jnp.mean(x * x, axis=1, keepdims=True) + EPSILON)
    part = width // CHUNKS
    for c in range(CHUNKS):
        cols = slice(c * part, (c + 1) * part)
        scaled = (tok_ref[:, cols].astype(F32) * inverse * gain_ref[:, cols]).astype(BF16)
        send[:, cols] = dot_nn(place, scaled).astype(BF16)
        put(c * part, (c + 1) * part)
    for copy in puts:
        copy.wait()


def dispatch(tokens, gain, ids, router, slots):
    tok_count, width = tokens.shape
    return pl.pallas_call(
        dispatch_kernel,
        grid=(1,),
        out_shape=(
            jax.ShapeDtypeStruct((slots, width + LANES), BF16),
            jax.ShapeDtypeStruct((slots, tok_count), BF16),
        ),
        in_specs=[whole((tok_count, width)), whole((1, width)), whole(ids.shape), whole(router.shape)],
        out_specs=(HBM, whole((slots, tok_count))),
        scratch_shapes=[pltpu.VMEM((slots, width + LANES), BF16), pltpu.SemaphoreType.DMA((1 + CHUNKS,))],
        compiler_params=pltpu.CompilerParams(dimension_semantics=("arbitrary",)),
        cost_estimate=cost(2 * slots * tok_count * width, 2 * slots * width * 2),
        name="dispatch_tokens",
    )(tokens, gain, ids, router)


def place_kernel(place_ref, x_ref, send_ref):
    send_ref[...] = dot_nn(place_ref[...], x_ref[...]).astype(BF16)


def place_rows(place, x):
    slots, tok_count = place.shape
    width = x.shape[1]
    chunks = 4
    part = width // chunks
    return pl.pallas_call(
        place_kernel,
        grid=(chunks,),
        out_shape=jax.ShapeDtypeStruct((slots, width), BF16),
        in_specs=[whole((slots, tok_count)), pl.BlockSpec((tok_count, part), lambda i: (0, i))],
        out_specs=pl.BlockSpec((slots, part), lambda i: (0, i)),
        compiler_params=pltpu.CompilerParams(dimension_semantics=("arbitrary",)),
        cost_estimate=cost(2 * slots * tok_count * width, 2 * slots * width * 2),
        name="dispatch_grads",
    )(place, x)


CHUNKS = 4


class Copies:
    def __init__(self, sems):
        self.sems = sems
        self.started = []

    def start(self, source, target):
        copy = pltpu.make_async_copy(source, target, self.sems.at[len(self.started)])
        copy.start()
        self.started.append(copy)
        return copy


def column_row(extra):
    rows_n, per_row = 8, 2
    stride = extra.shape[0] // rows_n
    parts = [extra[r * stride + j : r * stride + j + 1, :] for r in range(rows_n) for j in range(per_row)]
    return jnp.concatenate(parts, axis=1)


def forward_body(x_hbm, weights, sources, outs, scratch):
    wg, wu, wd = weights
    out_hbm, hg_hbm, fg_hbm, fu_hbm, gate_ref, rc_ref = outs
    block, hg, fg, fu, sems = scratch
    width = wd.shape[1]
    copies = Copies(sems)
    x, out = (x_hbm, block) if sources else (block, out_hbm)
    if not sources:
        copies.start(x_hbm, x).wait()
    got_w = [copies.start(source, target) for source, target in zip(sources, weights)]
    waits = lambda n: got_w[n].wait() if got_w else None
    rows = x[:, :width]
    row = column_row(x[:, width:].astype(F32))
    rc_ref[...] = jnp.broadcast_to(row, rc_ref.shape)
    gate = jax.nn.sigmoid(dot_nt(rows, jnp.broadcast_to(row, (LANES, width)).astype(BF16)))
    gate_ref[...] = gate
    gate = gate[:, :1]
    waits(0)
    g = dot_nt(rows, wg[...])
    waits(1)
    u = dot_nt(rows, wu[...])
    s = jax.nn.sigmoid(g)
    act = gate * (g * s)
    hg[...] = (act * u).astype(BF16)
    fu[...] = act.astype(BF16)
    fg[...] = (gate * s * u * (1.0 + g * (1.0 - s))).astype(BF16)
    puts = [copies.start(hg, hg_hbm), copies.start(fg, fg_hbm), copies.start(fu, fu_hbm)]
    waits(2)
    part = width // CHUNKS
    for c in range(CHUNKS):
        cols = slice(c * part, (c + 1) * part)
        out[:, cols] = dot_nn(hg[...], wd[:, cols]).astype(BF16)
        if sources:
            puts.append(copies.start(out.at[:, cols], out_hbm.at[:, cols]))
    for put in puts:
        put.wait()


def forward_loading_kernel(x_hbm, sg, su, sd, *refs):
    forward_body(x_hbm, refs[6:9], (sg, su, sd), refs[:6], refs[9:])


def forward_kernel(x_hbm, wg, wu, wd, *refs):
    forward_body(x_hbm, (wg, wu, wd), (), refs[:6], refs[6:])


def forward(x, weights, loading):
    rows = x.shape[0]
    ff, width = weights[0].shape
    outs = [
        jax.ShapeDtypeStruct((rows, width), BF16) if loading else pltpu.VMEM((rows, width), BF16),
        jax.ShapeDtypeStruct((rows, ff), BF16),
        jax.ShapeDtypeStruct((rows, ff), BF16),
        jax.ShapeDtypeStruct((rows, ff), BF16),
        jax.ShapeDtypeStruct((rows, LANES), F32),
        jax.ShapeDtypeStruct((CAP, width), F32),
    ]
    specs = [HBM if loading else VMEM] + [HBM] * 3 + [whole((rows, LANES)), whole((CAP, width))]
    if loading:
        outs += [pltpu.VMEM((ff, width), BF16)] * 3
        specs += [VMEM] * 3
    got = pl.pallas_call(
        forward_loading_kernel if loading else forward_kernel,
        grid=(1,),
        out_shape=tuple(outs),
        in_specs=[VMEM if loading else HBM] + [HBM if loading else VMEM] * 3,
        out_specs=tuple(specs),
        scratch_shapes=[
            pltpu.VMEM((rows, width) if loading else x.shape, BF16),
            pltpu.VMEM((rows, ff), BF16),
            pltpu.VMEM((rows, ff), BF16),
            pltpu.VMEM((rows, ff), BF16),
            pltpu.SemaphoreType.DMA((7 + CHUNKS,)),
        ],
        compiler_params=pltpu.CompilerParams(dimension_semantics=("arbitrary",), vmem_limit_bytes=KEEPING),
        cost_estimate=cost(6 * rows * ff * width, 6 * ff * width + 8 * rows * width),
        name="expert_forward",
    )(in_vmem(x) if loading else x, *weights)
    return got[:6], tuple(in_vmem(w) for w in got[6:])


def backward_body(ins, weights, sources, outs, scratch):
    wd, wg, wu = weights
    back_hbm, dg_hbm, du_hbm, gg_ref = outs
    block, hg, fg, fu, dg, du, sems = scratch
    width = wd.shape[1]
    copies = Copies(sems)
    gr, back = (ins[0], block) if sources else (block, back_hbm)
    got = [] if sources else [copies.start(ins[0], gr)]
    got_w = [copies.start(source, target) for source, target in zip(sources[:1], weights[:1])]
    got_more = [copies.start(source, target) for source, target in zip(ins[1:], (hg, fg, fu))]
    got_w += [copies.start(source, target) for source, target in zip(sources[1:], weights[1:])]
    waits = lambda n: got_w[n].wait() if got_w else None
    for copy in got:
        copy.wait()
    waits(0)
    dh = dot_nt(gr[...], wd[...])
    for copy in got_more:
        copy.wait()
    inner = jnp.sum(dh * hg[...].astype(F32), axis=1, keepdims=True)
    gg_ref[...] = jnp.broadcast_to(inner, gg_ref.shape)
    dg[...] = (dh * fg[...].astype(F32)).astype(BF16)
    du[...] = (dh * fu[...].astype(F32)).astype(BF16)
    puts = [copies.start(dg, dg_hbm), copies.start(du, du_hbm)]
    waits(1)
    waits(2)
    part = width // CHUNKS
    for c in range(CHUNKS):
        cols = slice(c * part, (c + 1) * part)
        back[:, cols] = (dot_nn(dg[...], wg[:, cols]) + dot_nn(du[...], wu[:, cols])).astype(BF16)
        if sources:
            puts.append(copies.start(back.at[:, cols], back_hbm.at[:, cols]))
    for put in puts:
        put.wait()


def backward_loading_kernel(gr, hg, fg, fu, sd, sg, su, *refs):
    backward_body((gr, hg, fg, fu), refs[4:7], (sd, sg, su), refs[:4], refs[7:])


def backward_kernel(gr, hg, fg, fu, wd, wg, wu, *refs):
    backward_body((gr, hg, fg, fu), (wd, wg, wu), (), refs[:4], refs[4:])


def backward(gr, hg, fg, fu, weights, loading):
    rows, width = gr.shape
    ff = weights[0].shape[0]
    outs = [
        jax.ShapeDtypeStruct((rows, width), BF16) if loading else pltpu.VMEM((rows, width), BF16),
        jax.ShapeDtypeStruct((rows, ff), BF16),
        jax.ShapeDtypeStruct((rows, ff), BF16),
        jax.ShapeDtypeStruct((rows, LANES), F32),
    ]
    specs = [HBM if loading else VMEM] + [HBM] * 2 + [whole((rows, LANES))]
    if loading:
        outs += [pltpu.VMEM((ff, width), BF16)] * 3
        specs += [VMEM] * 3
    got = pl.pallas_call(
        backward_loading_kernel if loading else backward_kernel,
        grid=(1,),
        out_shape=tuple(outs),
        in_specs=[VMEM if loading else HBM] + [HBM] * 3 + [HBM if loading else VMEM] * 3,
        out_specs=tuple(specs),
        scratch_shapes=[pltpu.VMEM((rows, width), BF16)]
        + [pltpu.VMEM((rows, ff), BF16)] * 3
        + [pltpu.VMEM((rows, ff), BF16)] * 2
        + [pltpu.SemaphoreType.DMA((9 + CHUNKS,))],
        compiler_params=pltpu.CompilerParams(dimension_semantics=("arbitrary",), vmem_limit_bytes=KEEPING),
        cost_estimate=cost(6 * rows * ff * width, 6 * ff * width + 8 * rows * width),
        name="expert_backward",
    )(in_vmem(gr) if loading else gr, hg, fg, fu, *weights)
    return got[:4], tuple(in_vmem(w) for w in got[4:])


def join_out_kernel(mine_ref, sib_ref, out_ref):
    rows = out_ref.shape[0]
    here = pl.ds(pl.multiple_of(pl.program_id(0) * rows, rows), rows)
    out_ref[...] = (mine_ref[here, :].astype(F32) + sib_ref[here, :].astype(F32)).astype(BF16)


def join_halves(mine, sib):
    rows, width = mine.shape
    blk = pl.BlockSpec((128, width), lambda i: (i, 0))
    return pl.pallas_call(
        join_out_kernel,
        grid=(rows // 128,),
        out_shape=jax.ShapeDtypeStruct((rows, width), BF16),
        in_specs=[VMEM, VMEM],
        out_specs=blk,
        compiler_params=pltpu.CompilerParams(dimension_semantics=("arbitrary",), vmem_limit_bytes=KEEPING),
        cost_estimate=cost(3 * rows * width, 6 * rows * width),
        name="join_halves",
    )(in_vmem(mine), in_vmem(sib))


def weight_grad_kernel(d0_ref, d1_ref, x0_ref, x1_ref, out_ref):
    out_ref[...] = (dot_tn(d0_ref[...], x0_ref[...]) + dot_tn(d1_ref[...], x1_ref[...])).astype(BF16)


def weight_grad(d0, d1, x0, x1, width):
    rows, ff = d0.shape
    part = 512
    col = pl.BlockSpec((rows, part), lambda i: (0, i))
    return pl.pallas_call(
        weight_grad_kernel,
        grid=(width // part,),
        out_shape=jax.ShapeDtypeStruct((ff, width), BF16),
        in_specs=[whole((rows, ff)), whole((rows, ff)), col, col],
        out_specs=pl.BlockSpec((ff, part), lambda i: (0, i)),
        compiler_params=pltpu.CompilerParams(dimension_semantics=("arbitrary",)),
        cost_estimate=cost(4 * rows * ff * width, 4 * rows * width + 2 * ff * width),
    )(d0, d1, x0, x1)


def join_kernel(mine_ref, sib_ref, gg_ref, gg_sib_ref, gate_ref, rc_ref, x_ref, back_ref, gain_scr, router_scr):
    step = pl.program_id(0)
    chunks, _, part = gain_scr.shape
    rows = back_ref.shape[0]

    @pl.when(step < chunks)
    def _():
        c = jnp.minimum(step, chunks - 1)
        gate = gate_ref[...]
        gl_wide = ((gg_ref[...] + gg_sib_ref[...]) * (1.0 - gate)).astype(BF16)
        gl = gl_wide.astype(F32)[:, :1]
        x = x_ref[...].astype(F32)
        here = pl.ds(pl.multiple_of(c * part, part), part)
        back = mine_ref[:, here].astype(F32) + sib_ref[:, here].astype(F32) + gl * rc_ref[:1, :]
        back_ref[...] = back.astype(BF16)
        gain_scr[c] = jnp.sum(x * back, axis=0, keepdims=True)
        router_scr[c] = dot_tn(gl_wide, x_ref[...])[:1, :]

    @pl.when(step == chunks)
    def _():
        lanes = chunks * part // CAP
        gain = jnp.concatenate([gain_scr[c] for c in range(chunks)], axis=1)
        gain = jnp.concatenate([gain[:, j * lanes : (j + 1) * lanes] for j in range(CAP)], axis=0)
        gain = jnp.broadcast_to(gain[None], (rows // CAP, CAP, lanes)).reshape(rows, lanes)
        back_ref[:, :lanes] = gain.astype(BF16)
        router = jnp.concatenate([router_scr[c] for c in range(chunks)], axis=1)
        parts = chunks * part // LANES
        router = jnp.concatenate([router[:, j * LANES : (j + 1) * LANES] for j in range(parts)], axis=0)
        per_row = parts // 8
        pick = one_hot_rows(
            rows,
            parts,
            lambda row: jnp.where(row % CAP < per_row, row // (rows // 8) * per_row + row % CAP, -1),
        )
        back_ref[:, lanes : lanes + LANES] = dot_nn(pick, router.astype(BF16)).astype(BF16)


def join_back(mine, sib, gg, gg_sib, gate, rc, x):
    rows, width = mine.shape
    part = 512
    chunks = width // part
    at = lambda i: (0, jnp.minimum(i, chunks - 1))
    col = pl.BlockSpec((rows, part), at)
    return pl.pallas_call(
        join_kernel,
        grid=(chunks + 1,),
        out_shape=jax.ShapeDtypeStruct((rows, width + width // CAP + LANES), BF16),
        in_specs=[VMEM, VMEM, whole((rows, LANES)), VMEM, whole((rows, LANES))] + [pl.BlockSpec((CAP, part), at), col],
        out_specs=pl.BlockSpec((rows, part), lambda i: (0, i)),
        scratch_shapes=[pltpu.VMEM((chunks, 1, part), F32), pltpu.VMEM((chunks, 1, part), F32)],
        compiler_params=pltpu.CompilerParams(dimension_semantics=("arbitrary",), vmem_limit_bytes=KEEPING),
        cost_estimate=cost(10 * rows * width, 8 * rows * width),
        name="join_back",
    )(in_vmem(mine), in_vmem(sib), gg, in_vmem(gg_sib), gate, rc, x)


def collect_kernel(a_ref, b_ref, c_ref, out_ref):
    rows = a_ref.shape[0]
    chips = rows // CAP
    for half, ref in enumerate((a_ref, b_ref)):
        total = jnp.sum(ref[...].astype(F32).reshape(chips, CAP, LANES), axis=0)
        out_ref[:CAP, half * LANES : (half + 1) * LANES] = total
    for j in range(2):
        pick = one_hot_rows(chips, rows, lambda row: row * CAP + j)
        out_ref[CAP:, j * LANES : (j + 1) * LANES] = dot_nn(pick, c_ref[...])


def collect(rows_in, width):
    rows = rows_in.shape[0]
    first = width // LANES
    lane = lambda k: pl.BlockSpec((rows, LANES), lambda i: (0, first + k))
    return pl.pallas_call(
        collect_kernel,
        grid=(1,),
        out_shape=jax.ShapeDtypeStruct((CAP + rows // CAP, 2 * LANES), F32),
        in_specs=[lane(0), lane(1), lane(2)],
        out_specs=whole((CAP + rows // CAP, 2 * LANES)),
        compiler_params=pltpu.CompilerParams(vmem_limit_bytes=50 << 20),
        cost_estimate=cost(rows * rows * LANES, 6 * rows * LANES),
        name="collect_sums",
    )(rows_in, rows_in, rows_in)


def total_kernel(mine_ref, sib_ref, gain_ref, gain_out_ref, router_ref):
    total = mine_ref[...] + sib_ref[...]
    router_ref[...] = total[CAP:, :]
    row = jnp.concatenate([total[j : j + 1, :] for j in range(CAP)], axis=1)
    gain_out_ref[...] = row / gain_ref[...]


def total_sums(mine, sib, gain):
    rows, part = mine.shape
    return pl.pallas_call(
        total_kernel,
        grid=(1,),
        out_shape=(
            jax.ShapeDtypeStruct(gain.shape, F32),
            jax.ShapeDtypeStruct((rows - CAP, part), F32),
        ),
        in_specs=[VMEM, VMEM, whole(gain.shape)],
        out_specs=(whole(gain.shape), whole((rows - CAP, part))),
        compiler_params=pltpu.CompilerParams(vmem_limit_bytes=50 << 20),
        cost_estimate=cost(2 * mine.size, 12 * mine.size),
        name="total_sums",
    )(in_vmem(mine), in_vmem(sib), gain)


def mix_kernel(place_ref, rows_ref, tok_ref, mixed_ref, acc_ref):
    step = pl.program_id(0)
    part = dot_tn(place_ref[...], rows_ref[...])

    @pl.when(step == 0)
    def _():
        acc_ref[...] = part

    @pl.when(step > 0)
    def _():
        acc_ref[...] += part

    @pl.when(step == pl.num_programs(0) - 1)
    def _():
        mixed_ref[...] = (tok_ref[...].astype(F32) + acc_ref[...]).astype(BF16)


def mix(place, rows, tokens):
    slots, tok_count = place.shape
    width = tokens.shape[1]
    part = 128
    return pl.pallas_call(
        mix_kernel,
        grid=(slots // part,),
        out_shape=jax.ShapeDtypeStruct((tok_count, width), BF16),
        in_specs=[
            pl.BlockSpec((part, tok_count), lambda i: (i, 0)),
            pl.BlockSpec((part, width), lambda i: (i, 0)),
            whole((tok_count, width)),
        ],
        out_specs=whole((tok_count, width)),
        scratch_shapes=[pltpu.VMEM((tok_count, width), F32)],
        compiler_params=pltpu.CompilerParams(dimension_semantics=("arbitrary",)),
        cost_estimate=cost(2 * slots * tok_count * width, 2 * slots * width),
        name="mix_outputs",
    )(place, rows, tokens)


def finish_kernel(place_ref, rows_ref, tok_ref, gain_ref, up_ref, out_ref, acc_ref):
    step = pl.program_id(0)
    part = dot_tn(place_ref[...], rows_ref[...])

    @pl.when(step == 0)
    def _():
        acc_ref[...] = part

    @pl.when(step > 0)
    def _():
        acc_ref[...] += part

    @pl.when(step == pl.num_programs(0) - 1)
    def _():
        x = tok_ref[...].astype(F32)
        inverse = lax.rsqrt(jnp.mean(x * x, axis=1, keepdims=True) + EPSILON)
        normed = x * inverse
        gn = acc_ref[...] * gain_ref[...]
        out = up_ref[...].astype(F32) + inverse * (gn - normed * jnp.mean(gn * normed, axis=1, keepdims=True))
        out_ref[...] = out.astype(BF16)


def finish(place, rows, tokens, gain, upstream):
    slots, tok_count = place.shape
    width = tokens.shape[1]
    part = 128
    return pl.pallas_call(
        finish_kernel,
        grid=(slots // part,),
        out_shape=jax.ShapeDtypeStruct((tok_count, width), BF16),
        in_specs=[
            pl.BlockSpec((part, tok_count), lambda i: (i, 0)),
            pl.BlockSpec((part, width), lambda i: (i, 0)),
            whole((tok_count, width)),
            whole((1, width)),
            whole((tok_count, width)),
        ],
        out_specs=whole((tok_count, width)),
        scratch_shapes=[pltpu.VMEM((tok_count, width), F32)],
        compiler_params=pltpu.CompilerParams(dimension_semantics=("arbitrary",), vmem_limit_bytes=50 << 20),
        cost_estimate=cost(2 * slots * tok_count * width, 2 * slots * width),
        name="finish_tokens",
    )(place, rows, tokens, gain, upstream)


def across(block, axis, bit):
    count = lax.axis_size(axis)
    return lax.ppermute(block, axis, [(i, i ^ bit) for i in range(count)])


def exchange(x, experts):
    rows, width = x.shape
    return lax.all_to_all(x.reshape(experts, -1, width), CHIPS, 0, 0, tiled=True).reshape(rows, width)


def local(tokens, norm_gain, router_weight, expert_ids, w_gate, w_up, w_down, grad_mixed):
    _, width = tokens.shape
    experts = router_weight.shape[1]
    slots = experts * CAP
    gain = norm_gain.reshape(1, width)
    wg, wu, wd = w_gate[0].T, w_up[0].T, w_down[0]

    send_in, place = dispatch(tokens, gain, expert_ids.T, router_weight.T, slots)
    in_0 = in_hbm(exchange(send_in, experts))
    send_grad = place_rows(place, grad_mixed)
    gr_0 = in_hbm(exchange(send_grad, experts))
    in_1 = across(in_0, CORE, 1)
    gr_1 = across(gr_0, CORE, 1)

    (out_1, hg_1, fg_1, fu_1, _, _), near = forward(in_1, (wg, wu, wd), True)
    (out_0, hg_0, fg_0, fu_0, gate_0, rc), _ = forward(in_0, near, False)
    out_s = across(out_1, CORE, 1)
    out = join_halves(out_0, out_s)
    got_out = in_hbm(exchange(out, experts))
    mixed = mix(place, got_out, tokens)

    (back_1, dg_1, du_1, gg_1), near = backward(gr_1, hg_1, fg_1, fu_1, (wd, wg, wu), True)
    (back_0, dg_0, du_0, gg_0), _ = backward(gr_0, hg_0, fg_0, fu_0, near, False)
    back_s = across(back_1, CORE, 1)
    gg_s = across(gg_1, CORE, 1)
    back = join_back(back_0, back_s, gg_0, gg_s, gate_0, rc, in_0)
    got_back = exchange(back, experts)
    grad_tokens = finish(place, got_back, tokens, gain, grad_mixed)

    grad_down = weight_grad(hg_0, hg_1, gr_0, gr_1, width)
    grad_gate = weight_grad(dg_0, dg_1, in_0, in_1, width)
    grad_up = weight_grad(du_0, du_1, in_0, in_1, width)

    sums = collect(got_back, width)
    sums_s = across(sums, CORE, 1)
    grad_gain, grad_router = total_sums(sums, sums_s, gain)
    return (
        mixed,
        grad_tokens,
        grad_gain.reshape(width),
        grad_router.T,
        grad_gate.T[None],
        grad_up.T[None],
        grad_down[None],
    )


def solution(mesh):
    finer = Mesh(mesh.devices.reshape(4, 2, 2, 4, 2), ROW_COL)
    placed = (
        P(ROW_COL, None),
        P(),
        P(ROW, None),
        P(ROW_COL, None),
        P(ROW_COL, None, None),
        P(ROW_COL, None, None),
        P(ROW_COL, None, None),
        P(ROW_COL, None),
    )
    return jax.shard_map(
        local,
        mesh=finer,
        in_specs=placed,
        out_specs=(
            P(ROW_COL, None),
            P(ROW_COL, None),
            P(),
            P(ROW, None),
            P(ROW_COL, None, None),
            P(ROW_COL, None, None),
            P(ROW_COL, None, None),
        ),
        check_vma=False,
    )
```

```python
import jax
import jax.numpy as jnp
from jax import lax
from jax.experimental import pallas as pl
from jax.experimental.pallas import tpu as pltpu
from jax.sharding import Mesh
from jax.sharding import PartitionSpec as P


ROW_COL = ("row_0", "row_1", "col_0", "col_1", "col_2")
CHIPS = ("row_0", "row_1", "col_0", "col_1")
ROW = ("row_0", "row_1")
CORE = "col_2"
CAP = 8
LANES = 128
F32 = jnp.float32
BF16 = jnp.bfloat16
EPSILON = 1e-06
KEEPING = 51 << 20
FINISHING = 50 << 20


def dot_nn(a, b):
    return lax.dot_general(a, b, (((1,), (0,)), ((), ())), preferred_element_type=F32)


def dot_nt(a, b):
    return lax.dot_general(a, b, (((1,), (1,)), ((), ())), preferred_element_type=F32)


def dot_tn(a, b):
    return lax.dot_general(a, b, (((0,), (0,)), ((), ())), preferred_element_type=F32)


VMEM = pl.BlockSpec(memory_space=pltpu.VMEM)
HBM = pl.BlockSpec(memory_space=pltpu.HBM)


def in_vmem(x):
    return pltpu.with_memory_space_constraint(x, pltpu.VMEM)


def in_hbm(x):
    return pltpu.with_memory_space_constraint(x, pltpu.HBM)


def cost(flops, bytes_accessed):
    return pl.CostEstimate(flops=int(flops), bytes_accessed=int(bytes_accessed), transcendentals=0)


def whole(shape):
    return pl.BlockSpec(shape, lambda i: (0,) * len(shape))


def one_hot_rows(rows, cols, column_of):
    row = lax.broadcasted_iota(jnp.int32, (rows, cols), 0)
    col = lax.broadcasted_iota(jnp.int32, (rows, cols), 1)
    return jnp.where(column_of(row) == col, 1.0, 0.0).astype(BF16)


def dispatch_kernel(tok_ref, gain_ref, ids_ref, router_ref, send_hbm, place_ref, send, sems):
    tok_count, width = tok_ref.shape
    slots = place_ref.shape[0]
    experts = slots // CAP
    puts = []

    def put(lo, hi):
        copy = pltpu.make_async_copy(send.at[:, lo:hi], send_hbm.at[:, lo:hi], sems.at[len(puts)])
        copy.start()
        puts.append(copy)

    ids = ids_ref[...]
    expert = lax.broadcasted_iota(jnp.int32, (experts, tok_count), 0)
    named = jnp.zeros((experts, tok_count), F32)
    for k in range(ids.shape[0]):
        named = named + jnp.where(ids[k : k + 1, :] == expert, 1.0, 0.0)
    before = lax.broadcasted_iota(jnp.int32, (tok_count, tok_count), 0)
    after = lax.broadcasted_iota(jnp.int32, (tok_count, tok_count), 1)
    earlier = jnp.where(before < after, 1.0, 0.0).astype(BF16)
    rank = dot_nn(named.astype(BF16), earlier)
    order = (named * (rank + 1.0)).astype(BF16)
    order_of = dot_nn(one_hot_rows(slots, experts, lambda row: row // CAP), order)
    want = (lax.broadcasted_iota(jnp.int32, (slots, tok_count), 0) % CAP + 1).astype(F32)
    place = jnp.where(order_of == want, 1.0, 0.0).astype(BF16)
    place_ref[...] = place
    extra = jnp.zeros((slots, LANES), F32)
    for j in range(router_ref.shape[1] // LANES):
        pick = one_hot_rows(slots, experts, lambda row: jnp.where(row % CAP == j, row // CAP, -1))
        extra = extra + dot_nn(pick, router_ref[:, j * LANES : (j + 1) * LANES])
    send[:, width:] = extra.astype(BF16)
    put(width, width + LANES)
    x = tok_ref[...].astype(F32)
    inverse = lax.rsqrt(jnp.mean(x * x, axis=1, keepdims=True) + EPSILON)
    part = width // CHUNKS
    for c in range(CHUNKS):
        cols = slice(c * part, (c + 1) * part)
        scaled = (tok_ref[:, cols].astype(F32) * inverse * gain_ref[:, cols]).astype(BF16)
        send[:, cols] = dot_nn(place, scaled).astype(BF16)
        put(c * part, (c + 1) * part)
    for copy in puts:
        copy.wait()


def dispatch(tokens, gain, ids, router, slots):
    tok_count, width = tokens.shape
    return pl.pallas_call(
        dispatch_kernel,
        grid=(1,),
        out_shape=(
            jax.ShapeDtypeStruct((slots, width + LANES), BF16),
            jax.ShapeDtypeStruct((slots, tok_count), BF16),
        ),
        in_specs=[whole((tok_count, width)), whole((1, width)), whole(ids.shape), whole(router.shape)],
        out_specs=(HBM, whole((slots, tok_count))),
        scratch_shapes=[pltpu.VMEM((slots, width + LANES), BF16), pltpu.SemaphoreType.DMA((1 + CHUNKS,))],
        compiler_params=pltpu.CompilerParams(dimension_semantics=("arbitrary",)),
        cost_estimate=cost(2 * slots * tok_count * width, 2 * slots * width * 2),
        name="dispatch_tokens",
    )(tokens, gain, ids, router)


def place_kernel(place_ref, x_ref, send_ref):
    send_ref[...] = dot_nn(place_ref[...], x_ref[...]).astype(BF16)


def place_rows(place, x):
    slots, tok_count = place.shape
    width = x.shape[1]
    chunks = 4
    part = width // chunks
    return pl.pallas_call(
        place_kernel,
        grid=(chunks,),
        out_shape=jax.ShapeDtypeStruct((slots, width), BF16),
        in_specs=[whole((slots, tok_count)), pl.BlockSpec((tok_count, part), lambda i: (0, i))],
        out_specs=pl.BlockSpec((slots, part), lambda i: (0, i)),
        compiler_params=pltpu.CompilerParams(dimension_semantics=("arbitrary",)),
        cost_estimate=cost(2 * slots * tok_count * width, 2 * slots * width * 2),
        name="dispatch_grads",
    )(place, x)


CHUNKS = 4


class Copies:
    def __init__(self, sems):
        self.sems = sems
        self.started = []

    def start(self, source, target):
        copy = pltpu.make_async_copy(source, target, self.sems.at[len(self.started)])
        copy.start()
        self.started.append(copy)
        return copy


def column_row(extra):
    rows_n, per_row = 8, 2
    stride = extra.shape[0] // rows_n
    parts = [extra[r * stride + j : r * stride + j + 1, :] for r in range(rows_n) for j in range(per_row)]
    return jnp.concatenate(parts, axis=1)


def forward_body(x_hbm, weights, sources, outs, scratch):
    wg, wu, wd = weights
    out_hbm, hg_hbm, fg_hbm, fu_hbm, gate_ref, rc_ref = outs
    block, hg, fg, fu, sems = scratch
    width = wd.shape[1]
    copies = Copies(sems)
    x, out = (x_hbm, block) if sources else (block, out_hbm)
    if not sources:
        copies.start(x_hbm, x).wait()
    got_w = [copies.start(source, target) for source, target in zip(sources, weights)]
    waits = lambda n: got_w[n].wait() if got_w else None
    rows = x[:, :width]
    row = column_row(x[:, width:].astype(F32))
    rc_ref[...] = jnp.broadcast_to(row, rc_ref.shape)
    gate = jax.nn.sigmoid(dot_nt(rows, jnp.broadcast_to(row, (LANES, width)).astype(BF16)))
    gate_ref[...] = gate
    gate = gate[:, :1]
    waits(0)
    g = dot_nt(rows, wg[...])
    waits(1)
    u = dot_nt(rows, wu[...])
    s = jax.nn.sigmoid(g)
    act = gate * (g * s)
    hg[...] = (act * u).astype(BF16)
    fu[...] = act.astype(BF16)
    fg[...] = (gate * s * u * (1.0 + g * (1.0 - s))).astype(BF16)
    puts = [copies.start(hg, hg_hbm), copies.start(fg, fg_hbm), copies.start(fu, fu_hbm)]
    waits(2)
    part = width // CHUNKS
    for c in range(CHUNKS):
        cols = slice(c * part, (c + 1) * part)
        out[:, cols] = dot_nn(hg[...], wd[:, cols]).astype(BF16)
        if sources:
            puts.append(copies.start(out.at[:, cols], out_hbm.at[:, cols]))
    for put in puts:
        put.wait()


def forward_loading_kernel(x_hbm, sg, su, sd, *refs):
    forward_body(x_hbm, refs[6:9], (sg, su, sd), refs[:6], refs[9:])


def forward_kernel(x_hbm, wg, wu, wd, *refs):
    forward_body(x_hbm, (wg, wu, wd), (), refs[:6], refs[6:])


def forward(x, weights, loading):
    rows = x.shape[0]
    ff, width = weights[0].shape
    outs = [
        jax.ShapeDtypeStruct((rows, width), BF16) if loading else pltpu.VMEM((rows, width), BF16),
        jax.ShapeDtypeStruct((rows, ff), BF16),
        jax.ShapeDtypeStruct((rows, ff), BF16),
        jax.ShapeDtypeStruct((rows, ff), BF16),
        jax.ShapeDtypeStruct((rows, LANES), F32),
        jax.ShapeDtypeStruct((CAP, width), F32),
    ]
    specs = [HBM if loading else VMEM] + [HBM] * 3 + [whole((rows, LANES)), whole((CAP, width))]
    if loading:
        outs += [pltpu.VMEM((ff, width), BF16)] * 3
        specs += [VMEM] * 3
    got = pl.pallas_call(
        forward_loading_kernel if loading else forward_kernel,
        grid=(1,),
        out_shape=tuple(outs),
        in_specs=[VMEM if loading else HBM] + [HBM if loading else VMEM] * 3,
        out_specs=tuple(specs),
        scratch_shapes=[
            pltpu.VMEM((rows, width) if loading else x.shape, BF16),
            pltpu.VMEM((rows, ff), BF16),
            pltpu.VMEM((rows, ff), BF16),
            pltpu.VMEM((rows, ff), BF16),
            pltpu.SemaphoreType.DMA((7 + CHUNKS,)),
        ],
        compiler_params=pltpu.CompilerParams(dimension_semantics=("arbitrary",), vmem_limit_bytes=KEEPING),
        cost_estimate=cost(6 * rows * ff * width, 6 * ff * width + 8 * rows * width),
        name="expert_forward",
    )(in_vmem(x) if loading else x, *weights)
    return got[:6], tuple(in_vmem(w) for w in got[6:])


def backward_body(ins, weights, sources, outs, scratch):
    wd, wg, wu = weights
    back_hbm, dg_hbm, du_hbm, gg_ref = outs
    block, hg, fg, fu, dg, du, sems = scratch
    width = wd.shape[1]
    copies = Copies(sems)
    gr, back = (ins[0], block) if sources else (block, back_hbm)
    got = [] if sources else [copies.start(ins[0], gr)]
    got_w = [copies.start(source, target) for source, target in zip(sources[:1], weights[:1])]
    got_more = [copies.start(source, target) for source, target in zip(ins[1:], (hg, fg, fu))]
    got_w += [copies.start(source, target) for source, target in zip(sources[1:], weights[1:])]
    waits = lambda n: got_w[n].wait() if got_w else None
    for copy in got:
        copy.wait()
    waits(0)
    dh = dot_nt(gr[...], wd[...])
    for copy in got_more:
        copy.wait()
    inner = jnp.sum(dh * hg[...].astype(F32), axis=1, keepdims=True)
    gg_ref[...] = jnp.broadcast_to(inner, gg_ref.shape)
    dg[...] = (dh * fg[...].astype(F32)).astype(BF16)
    du[...] = (dh * fu[...].astype(F32)).astype(BF16)
    puts = [copies.start(dg, dg_hbm), copies.start(du, du_hbm)]
    waits(1)
    waits(2)
    part = width // CHUNKS
    for c in range(CHUNKS):
        cols = slice(c * part, (c + 1) * part)
        back[:, cols] = (dot_nn(dg[...], wg[:, cols]) + dot_nn(du[...], wu[:, cols])).astype(BF16)
        if sources:
            puts.append(copies.start(back.at[:, cols], back_hbm.at[:, cols]))
    for put in puts:
        put.wait()


def backward_loading_kernel(gr, hg, fg, fu, sd, sg, su, *refs):
    backward_body((gr, hg, fg, fu), refs[4:7], (sd, sg, su), refs[:4], refs[7:])


def backward_kernel(gr, hg, fg, fu, wd, wg, wu, *refs):
    backward_body((gr, hg, fg, fu), (wd, wg, wu), (), refs[:4], refs[4:])


def backward(gr, hg, fg, fu, weights, loading):
    rows, width = gr.shape
    ff = weights[0].shape[0]
    outs = [
        jax.ShapeDtypeStruct((rows, width), BF16) if loading else pltpu.VMEM((rows, width), BF16),
        jax.ShapeDtypeStruct((rows, ff), BF16),
        jax.ShapeDtypeStruct((rows, ff), BF16),
        jax.ShapeDtypeStruct((rows, LANES), F32),
    ]
    specs = [HBM if loading else VMEM] + [HBM] * 2 + [whole((rows, LANES))]
    if loading:
        outs += [pltpu.VMEM((ff, width), BF16)] * 3
        specs += [VMEM] * 3
    got = pl.pallas_call(
        backward_loading_kernel if loading else backward_kernel,
        grid=(1,),
        out_shape=tuple(outs),
        in_specs=[VMEM if loading else HBM] + [HBM] * 3 + [HBM if loading else VMEM] * 3,
        out_specs=tuple(specs),
        scratch_shapes=[pltpu.VMEM((rows, width), BF16)]
        + [pltpu.VMEM((rows, ff), BF16)] * 3
        + [pltpu.VMEM((rows, ff), BF16)] * 2
        + [pltpu.SemaphoreType.DMA((9 + CHUNKS,))],
        compiler_params=pltpu.CompilerParams(dimension_semantics=("arbitrary",), vmem_limit_bytes=KEEPING),
        cost_estimate=cost(6 * rows * ff * width, 6 * ff * width + 8 * rows * width),
        name="expert_backward",
    )(in_vmem(gr) if loading else gr, hg, fg, fu, *weights)
    return got[:4], tuple(in_vmem(w) for w in got[4:])


def join_out_kernel(mine_ref, sib_ref, out_ref):
    rows = out_ref.shape[0]
    here = pl.ds(pl.multiple_of(pl.program_id(0) * rows, rows), rows)
    out_ref[...] = (mine_ref[here, :].astype(F32) + sib_ref[here, :].astype(F32)).astype(BF16)


def join_halves(mine, sib):
    rows, width = mine.shape
    blk = pl.BlockSpec((128, width), lambda i: (i, 0))
    return pl.pallas_call(
        join_out_kernel,
        grid=(rows // 128,),
        out_shape=jax.ShapeDtypeStruct((rows, width), BF16),
        in_specs=[VMEM, VMEM],
        out_specs=blk,
        compiler_params=pltpu.CompilerParams(dimension_semantics=("arbitrary",), vmem_limit_bytes=KEEPING),
        cost_estimate=cost(3 * rows * width, 6 * rows * width),
        name="join_halves",
    )(in_vmem(mine), in_vmem(sib))


def weight_grad_kernel(d0_ref, d1_ref, x0_ref, x1_ref, out_ref):
    out_ref[...] = (dot_tn(d0_ref[...], x0_ref[...]) + dot_tn(d1_ref[...], x1_ref[...])).astype(BF16)


def weight_grad(d0, d1, x0, x1, width):
    rows, ff = d0.shape
    part = 512
    col = pl.BlockSpec((rows, part), lambda i: (0, i))
    return pl.pallas_call(
        weight_grad_kernel,
        grid=(width // part,),
        out_shape=jax.ShapeDtypeStruct((ff, width), BF16),
        in_specs=[whole((rows, ff)), whole((rows, ff)), col, col],
        out_specs=pl.BlockSpec((ff, part), lambda i: (0, i)),
        compiler_params=pltpu.CompilerParams(dimension_semantics=("arbitrary",)),
        cost_estimate=cost(4 * rows * ff * width, 4 * rows * width + 2 * ff * width),
    )(d0, d1, x0, x1)


def join_kernel(mine_ref, sib_ref, gg_ref, gg_sib_ref, gate_ref, rc_ref, x_ref, back_ref, gain_scr, router_scr):
    step = pl.program_id(0)
    chunks, _, part = gain_scr.shape
    rows = back_ref.shape[0]

    @pl.when(step < chunks)
    def _():
        c = jnp.minimum(step, chunks - 1)
        gate = gate_ref[...]
        gl_wide = ((gg_ref[...] + gg_sib_ref[...]) * (1.0 - gate)).astype(BF16)
        gl = gl_wide.astype(F32)[:, :1]
        x = x_ref[...].astype(F32)
        here = pl.ds(pl.multiple_of(c * part, part), part)
        back = mine_ref[:, here].astype(F32) + sib_ref[:, here].astype(F32) + gl * rc_ref[:1, :]
        back_ref[...] = back.astype(BF16)
        gain_scr[c] = jnp.sum(x * back, axis=0, keepdims=True)
        router_scr[c] = dot_tn(gl_wide, x_ref[...])[:1, :]

    @pl.when(step == chunks)
    def _():
        lanes = chunks * part // CAP
        gain = jnp.concatenate([gain_scr[c] for c in range(chunks)], axis=1)
        gain = jnp.concatenate([gain[:, j * lanes : (j + 1) * lanes] for j in range(CAP)], axis=0)
        gain = jnp.broadcast_to(gain[None], (rows // CAP, CAP, lanes)).reshape(rows, lanes)
        back_ref[:, :lanes] = gain.astype(BF16)
        router = jnp.concatenate([router_scr[c] for c in range(chunks)], axis=1)
        parts = chunks * part // LANES
        router = jnp.concatenate([router[:, j * LANES : (j + 1) * LANES] for j in range(parts)], axis=0)
        per_row = parts // 8
        pick = one_hot_rows(
            rows,
            parts,
            lambda row: jnp.where(row % CAP < per_row, row // (rows // 8) * per_row + row % CAP, -1),
        )
        back_ref[:, lanes : lanes + LANES] = dot_nn(pick, router.astype(BF16)).astype(BF16)


def join_back(mine, sib, gg, gg_sib, gate, rc, x):
    rows, width = mine.shape
    part = 512
    chunks = width // part
    at = lambda i: (0, jnp.minimum(i, chunks - 1))
    col = pl.BlockSpec((rows, part), at)
    return pl.pallas_call(
        join_kernel,
        grid=(chunks + 1,),
        out_shape=jax.ShapeDtypeStruct((rows, width + width // CAP + LANES), BF16),
        in_specs=[VMEM, VMEM, whole((rows, LANES)), VMEM, whole((rows, LANES))] + [pl.BlockSpec((CAP, part), at), col],
        out_specs=pl.BlockSpec((rows, part), lambda i: (0, i)),
        scratch_shapes=[pltpu.VMEM((chunks, 1, part), F32), pltpu.VMEM((chunks, 1, part), F32)],
        compiler_params=pltpu.CompilerParams(dimension_semantics=("arbitrary",), vmem_limit_bytes=KEEPING),
        cost_estimate=cost(10 * rows * width, 8 * rows * width),
        name="join_back",
    )(in_vmem(mine), in_vmem(sib), gg, in_vmem(gg_sib), gate, rc, x)


def collect_kernel(a_ref, b_ref, c_ref, out_ref):
    rows = a_ref.shape[0]
    chips = rows // CAP
    for half, ref in enumerate((a_ref, b_ref)):
        total = jnp.sum(ref[...].astype(F32).reshape(chips, CAP, LANES), axis=0)
        out_ref[:CAP, half * LANES : (half + 1) * LANES] = total
    for j in range(2):
        pick = one_hot_rows(chips, rows, lambda row: row * CAP + j)
        out_ref[CAP:, j * LANES : (j + 1) * LANES] = dot_nn(pick, c_ref[...])


def collect(rows_in, width):
    rows = rows_in.shape[0]
    first = width // LANES
    lane = lambda k: pl.BlockSpec((rows, LANES), lambda i: (0, first + k))
    return pl.pallas_call(
        collect_kernel,
        grid=(1,),
        out_shape=jax.ShapeDtypeStruct((CAP + rows // CAP, 2 * LANES), F32),
        in_specs=[lane(0), lane(1), lane(2)],
        out_specs=whole((CAP + rows // CAP, 2 * LANES)),
        compiler_params=pltpu.CompilerParams(vmem_limit_bytes=FINISHING),
        cost_estimate=cost(rows * rows * LANES, 6 * rows * LANES),
        name="collect_sums",
    )(rows_in, rows_in, rows_in)


def total_kernel(mine_ref, sib_ref, gain_ref, gain_out_ref, router_ref):
    total = mine_ref[...] + sib_ref[...]
    router_ref[...] = total[CAP:, :]
    row = jnp.concatenate([total[j : j + 1, :] for j in range(CAP)], axis=1)
    gain_out_ref[...] = row / gain_ref[...]


def total_sums(mine, sib, gain):
    rows, part = mine.shape
    return pl.pallas_call(
        total_kernel,
        grid=(1,),
        out_shape=(
            jax.ShapeDtypeStruct(gain.shape, F32),
            jax.ShapeDtypeStruct((rows - CAP, part), F32),
        ),
        in_specs=[VMEM, VMEM, whole(gain.shape)],
        out_specs=(whole(gain.shape), whole((rows - CAP, part))),
        compiler_params=pltpu.CompilerParams(vmem_limit_bytes=FINISHING),
        cost_estimate=cost(2 * mine.size, 12 * mine.size),
        name="total_sums",
    )(in_vmem(mine), in_vmem(sib), gain)


def mix_kernel(place_ref, rows_ref, tok_ref, mixed_ref, acc_ref):
    step = pl.program_id(0)
    part = dot_tn(place_ref[...], rows_ref[...])

    @pl.when(step == 0)
    def _():
        acc_ref[...] = part

    @pl.when(step > 0)
    def _():
        acc_ref[...] += part

    @pl.when(step == pl.num_programs(0) - 1)
    def _():
        mixed_ref[...] = (tok_ref[...].astype(F32) + acc_ref[...]).astype(BF16)


def mix(place, rows, tokens):
    slots, tok_count = place.shape
    width = tokens.shape[1]
    part = 128
    return pl.pallas_call(
        mix_kernel,
        grid=(slots // part,),
        out_shape=jax.ShapeDtypeStruct((tok_count, width), BF16),
        in_specs=[
            pl.BlockSpec((part, tok_count), lambda i: (i, 0)),
            pl.BlockSpec((part, width), lambda i: (i, 0)),
            whole((tok_count, width)),
        ],
        out_specs=whole((tok_count, width)),
        scratch_shapes=[pltpu.VMEM((tok_count, width), F32)],
        compiler_params=pltpu.CompilerParams(dimension_semantics=("arbitrary",)),
        cost_estimate=cost(2 * slots * tok_count * width, 2 * slots * width),
        name="mix_outputs",
    )(place, rows, tokens)


def finish_kernel(place_ref, rows_ref, tok_ref, gain_ref, up_ref, out_ref, gn_scr):
    width = tok_ref.shape[1]
    part = width // CHUNKS
    x = tok_ref[...].astype(F32)
    inverse = lax.rsqrt(jnp.mean(x * x, axis=1, keepdims=True) + EPSILON)
    total = jnp.zeros(inverse.shape, F32)
    for c in range(CHUNKS):
        cols = slice(c * part, (c + 1) * part)
        gn = dot_tn(place_ref[...], rows_ref[:, cols]) * gain_ref[:, cols]
        gn_scr[:, cols] = gn
        total = total + jnp.sum(gn * (tok_ref[:, cols].astype(F32) * inverse), axis=1, keepdims=True)
    mean = total * (1.0 / width)
    for c in range(CHUNKS):
        cols = slice(c * part, (c + 1) * part)
        normed = tok_ref[:, cols].astype(F32) * inverse
        out = up_ref[:, cols].astype(F32) + inverse * (gn_scr[:, cols] - normed * mean)
        out_ref[:, cols] = out.astype(BF16)


def finish(place, rows, tokens, gain, upstream):
    slots, tok_count = place.shape
    width = tokens.shape[1]
    return pl.pallas_call(
        finish_kernel,
        grid=(1,),
        out_shape=jax.ShapeDtypeStruct((tok_count, width), BF16),
        in_specs=[
            whole((slots, tok_count)),
            VMEM,
            whole((tok_count, width)),
            whole((1, width)),
            whole((tok_count, width)),
        ],
        out_specs=whole((tok_count, width)),
        scratch_shapes=[pltpu.VMEM((tok_count, width), F32)],
        compiler_params=pltpu.CompilerParams(
            dimension_semantics=("arbitrary",), vmem_limit_bytes=FINISHING
        ),
        cost_estimate=cost(2 * slots * tok_count * width, 2 * slots * width),
        name="finish_tokens",
    )(place, in_vmem(rows), tokens, gain, upstream)


def across(block, axis, bit):
    count = lax.axis_size(axis)
    return lax.ppermute(block, axis, [(i, i ^ bit) for i in range(count)])


def exchange(x, experts):
    rows, width = x.shape
    return lax.all_to_all(x.reshape(experts, -1, width), CHIPS, 0, 0, tiled=True).reshape(rows, width)


def local(tokens, norm_gain, router_weight, expert_ids, w_gate, w_up, w_down, grad_mixed):
    _, width = tokens.shape
    experts = router_weight.shape[1]
    slots = experts * CAP
    gain = norm_gain.reshape(1, width)
    wg, wu, wd = w_gate[0].T, w_up[0].T, w_down[0]

    send_in, place = dispatch(tokens, gain, expert_ids.T, router_weight.T, slots)
    in_0 = in_hbm(exchange(send_in, experts))
    send_grad = place_rows(place, grad_mixed)
    gr_0 = in_hbm(exchange(send_grad, experts))
    in_1 = across(in_0, CORE, 1)
    gr_1 = across(gr_0, CORE, 1)

    (out_1, hg_1, fg_1, fu_1, _, _), near = forward(in_1, (wg, wu, wd), True)
    (out_0, hg_0, fg_0, fu_0, gate_0, rc), _ = forward(in_0, near, False)
    out_s = across(out_1, CORE, 1)
    out = join_halves(out_0, out_s)
    got_out = in_hbm(exchange(out, experts))
    mixed = mix(place, got_out, tokens)

    (back_1, dg_1, du_1, gg_1), near = backward(gr_1, hg_1, fg_1, fu_1, (wd, wg, wu), True)
    (back_0, dg_0, du_0, gg_0), _ = backward(gr_0, hg_0, fg_0, fu_0, near, False)
    back_s = across(back_1, CORE, 1)
    gg_s = across(gg_1, CORE, 1)
    back = join_back(back_0, back_s, gg_0, gg_s, gate_0, rc, in_0)
    got_back = exchange(back, experts)
    grad_tokens = finish(place, got_back, tokens, gain, grad_mixed)

    grad_down = weight_grad(hg_0, hg_1, gr_0, gr_1, width)
    grad_gate = weight_grad(dg_0, dg_1, in_0, in_1, width)
    grad_up = weight_grad(du_0, du_1, in_0, in_1, width)

    sums = collect(got_back, width)
    sums_s = across(sums, CORE, 1)
    grad_gain, grad_router = total_sums(sums, sums_s, gain)
    return (
        mixed,
        grad_tokens,
        grad_gain.reshape(width),
        grad_router.T,
        grad_gate.T[None],
        grad_up.T[None],
        grad_down[None],
    )


def solution(mesh):
    finer = Mesh(mesh.devices.reshape(4, 2, 2, 4, 2), ROW_COL)
    placed = (
        P(ROW_COL, None),
        P(),
        P(ROW, None),
        P(ROW_COL, None),
        P(ROW_COL, None, None),
        P(ROW_COL, None, None),
        P(ROW_COL, None, None),
        P(ROW_COL, None),
    )
    return jax.shard_map(
        local,
        mesh=finer,
        in_specs=placed,
        out_specs=(
            P(ROW_COL, None),
            P(ROW_COL, None),
            P(),
            P(ROW, None),
            P(ROW_COL, None, None),
            P(ROW_COL, None, None),
            P(ROW_COL, None, None),
        ),
        check_vma=False,
    )
```
